32 devices in a mesh: dp: 8 (over y, x, core), tensor: 4 (over z).
Axes of the slice: x: 2, y: 2, z: 4, core: 2. Of those that a mesh axis runs over, the one named last changes fastest.
Arguments:
- tokens: bfloat16 [8192, 2048], P('dp'), may hold values from -6 to 6
- positions: int32 [8, 1024], P('dp'), may hold values from 0 to 2046, as said below
- span_starts: int32 [8, 2], P('dp'), may hold values from 0 to 768, as said below
- attention_gain: bfloat16 [2048], replicated, may hold values from 0.099609375 to 1.8984375
- query_weight: bfloat16 [2048, 2048], P(None, 'tensor'), may hold values from -0.125 to 0.125
- key_matrix: bfloat16 [2048, 1024], P(None, 'tensor'), may hold values from -0.125 to 0.125
- value_matrix: bfloat16 [2048, 1024], P(None, 'tensor'), may hold values from -0.125 to 0.125
- query_gain: bfloat16 [128], replicated, may hold values from 0.5 to 2
- key_gain: bfloat16 [128], replicated, may hold values from 0.5 to 2
- output_weight: bfloat16 [2048, 2048], P('tensor'), may hold values from -1 to 1
- feedforward_gain: bfloat16 [2048], replicated, may hold values from 0.099609375 to 1.8984375
- gate_weight: bfloat16 [2048, 6144], P(None, 'tensor'), may hold values from -0.125 to 0.125
- up_weight: bfloat16 [2048, 6144], P(None, 'tensor'), may hold values from -0.125 to 0.125
- down_weight: bfloat16 [6144, 2048], P('tensor'), may hold values from -0.078125 to 0.078125
- cotangent: bfloat16 [8192, 2048], P('dp'), may hold values from -6 to 6
Outputs:
- block_output: bfloat16 [8192, 2048], P('dp')
- tokens_grad: bfloat16 [8192, 2048], P('dp')
- attention_gain_grad: float32 [2048], P('dp')
- query_weight_grad: float32 [2048, 2048], P('dp', 'tensor')
- key_weight_grad: float32 [2048, 1024], P('dp', 'tensor')
- value_weight_grad: float32 [2048, 1024], P('dp', 'tensor')
- query_gain_grad: float32 [128], P('dp')
- key_gain_grad: float32 [128], P('dp')
- output_weight_grad: float32 [2048, 2048], P('tensor', 'dp')
- feedforward_gain_grad: float32 [2048], P('dp')
- gate_weight_grad: float32 [2048, 6144], P('dp', 'tensor')
- up_weight_grad: float32 [2048, 6144], P('dp', 'tensor')
- down_weight_grad: float32 [6144, 2048], P('tensor', 'dp')
The draws below stay inside these ranges and needn't reach their ends.
Inputs may be any that keep to these rules, and one draw needn't show every extreme that they name: Within each sequence positions start at 0 and rise by 1 or 2 from one token to the next. `span_starts`: each sequence has two picture spans of 256 tokens: the first starts and ends within the first 512 tokens, the second starts at 512 or later and ends inside the sequence.
All inputs are finite; a program needn't handle non-finite values.
Results may differ from the reference program's by a relative error of at most 0.015.
Values sent between devices are 32-bit elements; how exact they have to be, the bound alone decides.
No kernel may reach another device: no remote copies, remote signals or barrier semaphores. Data moves between devices by JAX's collectives and lax.ppermute only.
A program may use at most 256 MiB of HBM per device.

```python
import math
import jax
import jax.numpy as jnp
from jax import lax

MODEL_WIDTH = 2048
QUERY_HEADS = 16
KEY_VALUE_HEADS = 8
HEAD_WIDTH = 128
FF = 6144
SEQUENCE_LENGTH = 1024
SPAN = 256
SEQS = 8
TOKENS = 8192


def draw_positions(key, part):
    steps_up = jax.random.randint(jax.random.fold_in(key, 11), (SEQS, SEQUENCE_LENGTH), 1, 3, dtype=jnp.int32)
    row_index = jnp.arange(SEQS, dtype=jnp.int32)[:, None]
    steps_up = jnp.where(row_index == SEQS - 1, 2, steps_up).astype(jnp.int32)
    climbed = jnp.cumsum(steps_up, axis=1)
    return (climbed - climbed[:, :1]).astype(jnp.int32)


def draw_span_starts(key, part):
    start_room = SEQUENCE_LENGTH // 2 - SPAN + 1
    first_start = jax.random.randint(jax.random.fold_in(key, 21), (SEQS, 1), 0, start_room, dtype=jnp.int32)
    second_start = SEQUENCE_LENGTH // 2 + jax.random.randint(jax.random.fold_in(key, 22), (SEQS, 1), 0, start_room, dtype=jnp.int32)
    row_index = jnp.arange(SEQS, dtype=jnp.int32)[:, None]
    first_start = jnp.where(row_index == 0, 0, first_start).astype(jnp.int32)
    second_start = jnp.where(row_index == 0, SEQUENCE_LENGTH - SPAN, second_start).astype(jnp.int32)
    return jnp.concatenate([first_start, second_start], axis=1).astype(jnp.int32)


def spiked(entries, rng, source, target, parts, factor):
    owner, partner = [(jnp.arange(entries.shape[dim]) // (entries.shape[dim] // parts)).reshape([-1 if axis == dim else 1 for axis in range(entries.ndim)]) for dim in (source, target)]
    chosen = jax.random.permutation(rng, parts)[partner]
    strong = (owner == chosen) | (owner == (partner + parts // 2) % parts)
    return jnp.where(strong, factor * entries, entries)


def levels(key, shape, shards, least, high):
    loudness, own = 1.0, jax.random.fold_in(key, 6)
    for axis_at, blocks in shards:
        heights = jnp.exp(jax.random.uniform(jax.random.fold_in(own, axis_at), (blocks,), jnp.float32, least / len(shards), high / len(shards)))
        loudness = loudness * jnp.repeat(heights, shape[axis_at] // blocks).reshape([-1 if axis == axis_at else 1 for axis in range(len(shape))])
    return loudness


def gaussian(rng, shape, spread, bound, cuts=(), kind=jnp.bfloat16):
    level = levels(rng, shape, cuts, -0.22, 0.18) if cuts else 1.0
    array = jax.random.normal(rng, shape, jnp.float32) * spread * level
    return jnp.minimum(jnp.maximum(array, -bound), bound).astype(kind)


def bell_draw_with(stream_key, extent, deviation, limit, split, heavy, kind=jnp.bfloat16):
    values = deviation * jax.random.normal(stream_key, extent, jnp.float32)
    if split:
        values = values * levels(stream_key, extent, split, -0.22, 0.18)
    return jnp.clip(spiked(values, jax.random.fold_in(stream_key, 3), *heavy), -limit, limit).astype(kind)


def setup_inputs(seed: int = 0) -> dict:
    streams_of = jax.random.split(jax.random.key(seed), 16)
    return {
        "tokens": bell_draw_with(streams_of[0], (TOKENS, MODEL_WIDTH), 1.0, 6.0, ((0, 8),), (0, 1, 8, 2.0)),
        "positions": draw_positions(jax.random.fold_in(streams_of[15], 71), 0),
        "span_starts": draw_span_starts(jax.random.fold_in(streams_of[15], 71), 0),
        "attention_gain": jnp.clip(1.0 + 0.18 * jax.random.normal(streams_of[3], (MODEL_WIDTH,), jnp.float32), 0.099609375, 1.8984375).astype(jnp.bfloat16),
        "query_weight": gaussian(streams_of[4], (MODEL_WIDTH, QUERY_HEADS * HEAD_WIDTH), MODEL_WIDTH ** -0.5, 0.125, ((1, 4),)),
        "key_matrix": gaussian(streams_of[5], (MODEL_WIDTH, KEY_VALUE_HEADS * HEAD_WIDTH), MODEL_WIDTH ** -0.5, 0.125, ((1, 4),)),
        "value_matrix": gaussian(streams_of[6], (MODEL_WIDTH, KEY_VALUE_HEADS * HEAD_WIDTH), MODEL_WIDTH ** -0.5, 0.125, ((1, 4),)),
        "query_gain": jnp.clip(jax.random.uniform(streams_of[7], (HEAD_WIDTH,), jnp.float32, 0.5, 2.0), 0.5, 2.0).astype(jnp.bfloat16),
        "key_gain": jnp.clip(jax.random.uniform(streams_of[8], (HEAD_WIDTH,), jnp.float32, 0.5, 2.0), 0.5, 2.0).astype(jnp.bfloat16),
        "output_weight": gaussian(streams_of[9], (QUERY_HEADS * HEAD_WIDTH, MODEL_WIDTH), (QUERY_HEADS * HEAD_WIDTH // 64) ** -0.5, 1.0, ((0, 4),)),
        "feedforward_gain": jnp.clip(1.0 + 0.18 * jax.random.normal(streams_of[10], (MODEL_WIDTH,), jnp.float32), 0.099609375, 1.8984375).astype(jnp.bfloat16),
        "gate_weight": gaussian(streams_of[11], (MODEL_WIDTH, FF), MODEL_WIDTH ** -0.5, 0.125, ((1, 4),)),
        "up_weight": gaussian(streams_of[12], (MODEL_WIDTH, FF), MODEL_WIDTH ** -0.5, 0.125, ((1, 4),)),
        "down_weight": gaussian(streams_of[13], (FF, MODEL_WIDTH), FF ** -0.5, 0.078125, ((0, 4),)),
        "cotangent": bell_draw_with(streams_of[14], (TOKENS, MODEL_WIDTH), 1.0, 6.0, ((0, 8),), (0, 1, 8, 2.0)),
    }


epsilon = 1e-06
rope_base = 1000000.0

@jax.custom_vjp
def to_bfloat(v):
    return lax.optimization_barrier(v.astype(jnp.bfloat16)).astype(jnp.float32)

@jax.custom_vjp
def to_bfloat_back(v):
    return v

def low_keep(v):
    return (to_bfloat(v), None)

def low_pass(kept, grad):
    return (grad,)

def back_keep(v):
    return (v, None)

def back_low(kept, grad):
    return (to_bfloat(grad),)
to_bfloat.defvjp(low_keep, low_pass)
to_bfloat_back.defvjp(back_keep, back_low)

def product_highest(left, right):
    return jnp.dot(left, right, precision=lax.Precision.HIGHEST, preferred_element_type=jnp.float32)

def rms_scale(values, gain):
    factor = lax.rsqrt(lax.optimization_barrier(jnp.mean(values * values, axis=-1, keepdims=True)) + epsilon)
    return values * factor * gain

def rotate_half(values, cosine, sine):
    half_size = values.shape[-1] // 2
    first_half = values[..., :half_size]
    second_half = values[..., half_size:]
    return jnp.concatenate([first_half * cosine - second_half * sine, second_half * cosine + first_half * sine], axis=-1)

def span_mask(starts):
    token_index = jnp.arange(SEQUENCE_LENGTH, dtype=jnp.int32)
    inside = (token_index[None, None, :] >= starts[:, :, None]) & (token_index[None, None, :] < starts[:, :, None] + SPAN)
    span_number = jnp.arange(starts.shape[1], dtype=jnp.int32)[None, :, None] + 1
    span_label = lax.optimization_barrier(jnp.sum(inside.astype(jnp.int32) * span_number, axis=1))
    causal = token_index[:, None] >= token_index[None, :]
    same_span = (span_label[:, :, None] == span_label[:, None, :]) & (span_label[:, :, None] > 0)
    return causal[None] | same_span

def layer_group(params, x_group, pos_group, start_group):
    attention_gain, query_weight, key_matrix, value_matrix, query_gain, key_gain, output_weight, feedforward_gain, gate_weight, up_weight, down_weight = params
    group_count = x_group.shape[0]
    flat_rows = x_group.reshape(group_count * SEQUENCE_LENGTH, MODEL_WIDTH)
    normalized_rows = to_bfloat(rms_scale(flat_rows, attention_gain))
    query_raw = to_bfloat_back(product_highest(normalized_rows, query_weight)).reshape(group_count, SEQUENCE_LENGTH, QUERY_HEADS, HEAD_WIDTH)
    key_unrotated = to_bfloat_back(product_highest(normalized_rows, key_matrix)).reshape(group_count, SEQUENCE_LENGTH, KEY_VALUE_HEADS, HEAD_WIDTH)
    heads_value = to_bfloat(to_bfloat_back(product_highest(normalized_rows, value_matrix))).reshape(group_count, SEQUENCE_LENGTH, KEY_VALUE_HEADS, HEAD_WIDTH)
    frequency = jnp.exp(jnp.arange(HEAD_WIDTH // 2, dtype=jnp.float32) * (-2.0 * math.log(rope_base) / HEAD_WIDTH))
    angles = pos_group.astype(jnp.float32)[:, :, None] * frequency
    cosine = jnp.cos(angles)[:, :, None, :]
    sine = jnp.sin(angles)[:, :, None, :]
    query_rows = to_bfloat(rotate_half(rms_scale(query_raw, query_gain), cosine, sine))
    key_heads = to_bfloat(rotate_half(rms_scale(key_unrotated, key_gain), cosine, sine))
    grouped_heads = query_rows.reshape(group_count, SEQUENCE_LENGTH, KEY_VALUE_HEADS, QUERY_HEADS // KEY_VALUE_HEADS, HEAD_WIDTH)
    scores = jnp.einsum('bqhgd,bkhd->bhgqk', grouped_heads, key_heads, precision=lax.Precision.HIGHEST)
    scores = to_bfloat_back(scores * HEAD_WIDTH ** (-0.5))
    scores = jnp.where(span_mask(start_group)[:, None, None], scores, -jnp.inf)
    highest = lax.optimization_barrier(jnp.max(scores, axis=-1, keepdims=True))
    exponent = jnp.exp(scores - highest)
    probability = to_bfloat(exponent / lax.optimization_barrier(jnp.sum(exponent, axis=-1, keepdims=True)))
    mixed_heads = jnp.einsum('bhgqk,bkhd->bqhgd', probability, heads_value, precision=lax.Precision.HIGHEST)
    mixed_heads = to_bfloat(to_bfloat_back(mixed_heads.reshape(group_count * SEQUENCE_LENGTH, QUERY_HEADS * HEAD_WIDTH)))
    residual = flat_rows + to_bfloat_back(product_highest(mixed_heads, output_weight))
    normed_two = to_bfloat(rms_scale(residual, feedforward_gain))
    gate_values = to_bfloat_back(product_highest(normed_two, gate_weight))
    up_values = to_bfloat_back(product_highest(normed_two, up_weight))
    hidden = to_bfloat(jax.nn.silu(gate_values) * up_values)
    block_rows = residual + to_bfloat_back(product_highest(hidden, down_weight))
    return block_rows.reshape(group_count, SEQUENCE_LENGTH, MODEL_WIDTH)

def reference(tokens, positions, span_starts, attention_gain, query_weight, key_matrix, value_matrix, query_gain, key_gain, output_weight, feedforward_gain, gate_weight, up_weight, down_weight, cotangent):
    params = tuple((weight.astype(jnp.float32) for weight in (attention_gain, query_weight, key_matrix, value_matrix, query_gain, key_gain, output_weight, feedforward_gain, gate_weight, up_weight, down_weight)))
    group_size = math.gcd(SEQS, max(1, 4096 // SEQUENCE_LENGTH))
    blocks = SEQS // group_size
    x_blocks = tokens.astype(jnp.float32).reshape(blocks, group_size, SEQUENCE_LENGTH, MODEL_WIDTH)
    pos_blocks = positions.reshape(blocks, group_size, SEQUENCE_LENGTH)
    start_blocks = span_starts.reshape(blocks, group_size, 2)

    def forward(x_all, weights):

        def scan_step(carried, sequence_items):
            return (carried, layer_group(weights, sequence_items[0], sequence_items[1], sequence_items[2]))
        carried, result = lax.scan(jax.checkpoint(scan_step), jnp.zeros((), jnp.float32), (x_all, pos_blocks, start_blocks))
        return result
    result, pullback = jax.vjp(forward, x_blocks, params)
    x_grad, weight_grads = pullback(cotangent.astype(jnp.float32).reshape(blocks, group_size, SEQUENCE_LENGTH, MODEL_WIDTH))
    return (result.reshape(TOKENS, MODEL_WIDTH).astype(jnp.bfloat16), x_grad.reshape(TOKENS, MODEL_WIDTH).astype(jnp.bfloat16), weight_grads[0], weight_grads[1], weight_grads[2], weight_grads[3], weight_grads[4], weight_grads[5], weight_grads[6], weight_grads[7], weight_grads[8], weight_grads[9], weight_grads[10])
```

```python
import math

import jax
import jax.numpy as jnp
from jax import lax
from jax.sharding import PartitionSpec as P

SPAN = 256
HALF = 512

epsilon = 1e-06
rope_base = 1000000.0


def contract(left, right, left_dim, right_dim):
    return lax.dot_general(
        left, right, (((left_dim,), (right_dim,)), ((), ())), preferred_element_type=jnp.float32
    )


def norm_rows(values, gain):
    factor = lax.rsqrt(jnp.mean(values * values, axis=-1, keepdims=True) + epsilon)
    return (values * factor * gain, factor)


def norm_back(values, factor, gain, grad_out):
    scaled = grad_out * gain
    inner_sum = jnp.sum(scaled * values, axis=-1, keepdims=True)
    grad_in = factor * scaled - values * (factor * factor * factor) * inner_sum / values.shape[-1]
    return (grad_in, grad_out * values * factor)


def rotate_half(values, cosine, sine):
    half_size = values.shape[-1] // 2
    first_half = values[..., :half_size]
    second_half = values[..., half_size:]
    return jnp.concatenate(
        [first_half * cosine - second_half * sine, second_half * cosine + first_half * sine],
        axis=-1,
    )


def rotate_back(values, cosine, sine):
    half_size = values.shape[-1] // 2
    first_half = values[..., :half_size]
    second_half = values[..., half_size:]
    return jnp.concatenate(
        [first_half * cosine + second_half * sine, second_half * cosine - first_half * sine],
        axis=-1,
    )


def span_mask(starts, seq_length):
    token_index = jnp.arange(seq_length, dtype=jnp.int32)
    inside = (token_index[None, :] >= starts[:, None]) & (
        token_index[None, :] < starts[:, None] + SPAN
    )
    span_number = jnp.arange(starts.shape[0], dtype=jnp.int32)[:, None] + 1
    span_label = jnp.sum(inside.astype(jnp.int32) * span_number, axis=0)
    causal = token_index[:, None] >= token_index[None, :]
    same_span = (span_label[:, None] == span_label[None, :]) & (span_label[:, None] > 0)
    return causal | same_span


def score_block(query_rows, key_heads, allowed, score_scale):
    scores = (
        jnp.einsum("qhgd,khd->hgqk", query_rows, key_heads, preferred_element_type=jnp.float32)
        * score_scale
    )
    return jnp.where(allowed, scores, -jnp.inf)


def attend(query_rows, key_heads, heads_value, allowed, score_scale):
    scores = score_block(query_rows, key_heads, allowed, score_scale)
    highest = jnp.max(scores, axis=-1, keepdims=True)
    exponent = jnp.exp(scores - highest)
    denominator = jnp.sum(exponent, axis=-1, keepdims=True)
    probability = (exponent / denominator).astype(jnp.bfloat16)
    mixed_heads = jnp.einsum(
        "hgqk,khd->qhgd", probability, heads_value, preferred_element_type=jnp.float32
    )
    return (mixed_heads, (highest + jnp.log(denominator))[..., 0])


def attend_back(query_rows, key_heads, heads_value, allowed, log_total, grad_mixed, score_scale):
    scores = score_block(query_rows, key_heads, allowed, score_scale)
    probability = jnp.exp(scores - log_total[..., None])
    grad_value = jnp.einsum(
        "hgqk,qhgd->khd",
        probability.astype(jnp.bfloat16),
        grad_mixed,
        preferred_element_type=jnp.float32,
    )
    grad_prob = jnp.einsum(
        "qhgd,khd->hgqk", grad_mixed, heads_value, preferred_element_type=jnp.float32
    )
    grad_scores = probability * (
        grad_prob - jnp.sum(probability * grad_prob, axis=-1, keepdims=True)
    )
    grad_low = grad_scores.astype(jnp.bfloat16)
    grad_queries = (
        jnp.einsum("hgqk,khd->qhgd", grad_low, key_heads, preferred_element_type=jnp.float32)
        * score_scale
    )
    grad_keys = (
        jnp.einsum("hgqk,qhgd->khd", grad_low, query_rows, preferred_element_type=jnp.float32)
        * score_scale
    )
    return (grad_queries, grad_keys, grad_value)


def chain_gather(block, count, place):
    upward = block
    downward = block
    from_below = [block]
    from_above = [block]
    for step in range(1, count):
        upward = lax.ppermute(upward, "tensor", [(i, i + 1) for i in range(step - 1, count - 1)])
        downward = lax.ppermute(downward, "tensor", [(i, i - 1) for i in range(1, count - step + 1)])
        from_below.append(upward)
        from_above.append(downward)
    return [block] + [
        jnp.where(place >= slot, from_below[slot], from_above[count - slot])
        for slot in range(1, count)
    ]


def chain_reduce(parts, count):
    upward = parts[count - 1]
    downward = parts[1 % count]
    for step in range(1, count):
        upward = lax.ppermute(upward, "tensor", [(i, i + 1) for i in range(step)])
        downward = lax.ppermute(downward, "tensor", [(i, i - 1) for i in range(count - step, count)])
        if step < count - 1:
            upward = upward + parts[count - 1 - step]
            downward = downward + parts[step + 1]
    return parts[0] + upward + downward


def row_block(values, start, rows):
    return lax.dynamic_slice_in_dim(values, start, rows, axis=0)


def shards(
    tokens,
    positions,
    span_starts,
    attention_gain,
    query_weight,
    key_matrix,
    value_matrix,
    query_gain,
    key_gain,
    output_weight,
    feedforward_gain,
    gate_weight,
    up_weight,
    down_weight,
    cotangent,
):
    low = jnp.bfloat16
    ranks = lax.axis_size("tensor")
    groups = lax.axis_size("dp")
    place = lax.axis_index("tensor")
    group = lax.axis_index("dp")
    seq_count, seq_length = positions.shape
    head_size = query_gain.shape[0]
    local_width = query_weight.shape[1]
    model_width = query_weight.shape[0]
    query_heads = local_width // head_size
    kv_heads = key_matrix.shape[1] // head_size
    group_size = query_heads // kv_heads
    token_count = seq_count * seq_length
    score_scale = head_size ** (-0.5)
    attention_gain_f = attention_gain.astype(jnp.float32)
    feedforward_gain_f = feedforward_gain.astype(jnp.float32)
    query_gain_f = query_gain.astype(jnp.float32)
    key_gain_f = key_gain.astype(jnp.float32)

    unit = jnp.where(positions[0, 0] >= 0, 1.0, 0.0)

    weight_rows = local_width // groups
    own_rows = row_block(output_weight, group * weight_rows, weight_rows).astype(jnp.float32)
    whole_weight = lax.all_gather(own_rows, ("tensor", "dp"), axis=0, tiled=True)
    whole_weight = (whole_weight * unit).astype(low)

    inputs = tokens.astype(jnp.float32)
    normalized_rows, factor_one = norm_rows(inputs, attention_gain_f)
    normed_low = normalized_rows.astype(low)
    query_raw = jnp.dot(normed_low, query_weight, preferred_element_type=jnp.float32).reshape(
        token_count, query_heads, head_size
    )
    key_unrotated = jnp.dot(normed_low, key_matrix, preferred_element_type=jnp.float32).reshape(
        token_count, kv_heads, head_size
    )
    value_low = jnp.dot(normed_low, value_matrix, preferred_element_type=jnp.float32).astype(low)
    frequency = jnp.exp(
        jnp.arange(head_size // 2, dtype=jnp.float32) * (-2.0 * math.log(rope_base) / head_size)
    )
    angles = positions.astype(jnp.float32).reshape(token_count)[:, None] * frequency
    cosine = jnp.cos(angles)[:, None, :]
    sine = jnp.sin(angles)[:, None, :]
    query_normed, query_factor = norm_rows(query_raw, query_gain_f)
    key_normed, key_factor = norm_rows(key_unrotated, key_gain_f)
    query_low = rotate_half(query_normed, cosine, sine).astype(low)
    key_low = rotate_half(key_normed, cosine, sine).astype(low)
    query_all = query_low.reshape(token_count, kv_heads, group_size, head_size)
    key_all = key_low.reshape(token_count, kv_heads, head_size)
    value_all = value_low.reshape(token_count, kv_heads, head_size)

    streams = []
    for sequence in range(seq_count):
        base = sequence * seq_length
        streams.append((sequence, base, base + HALF, base + HALF))
        streams.append((sequence, base + HALF, base + seq_length, base + seq_length))
    masks = [span_mask(span_starts[sequence], seq_length) for sequence in range(seq_count)]

    def keys_of(stream):
        sequence, first, end, key_end = stream
        return slice(sequence * seq_length, key_end)

    def mask_of(stream):
        sequence, first, end, key_end = stream
        base = sequence * seq_length
        return masks[sequence][first - base : end - base, : key_end - base]

    state = []
    for stream in streams:
        sequence, first, end, key_end = stream
        keys = keys_of(stream)
        mixed, log_total = attend(
            query_all[first:end], key_all[keys], value_all[keys], mask_of(stream), score_scale
        )
        rows = end - first
        gathered = lax.all_gather(mixed.reshape(rows, local_width), "tensor", axis=0)
        gathered = (gathered * unit).astype(low)
        mixed_whole = gathered.transpose(1, 0, 2).reshape(rows, ranks * local_width)
        state.append({"stream": stream, "log_total": log_total, "mixed": mixed_whole})

    grad_hidden = contract(cotangent, down_weight, 1, 1)

    for item in state:
        _, first, end, _ = item["stream"]
        rows = end - first
        share = rows // ranks
        residual = inputs[first:end] + jnp.dot(
            item["mixed"], whole_weight, preferred_element_type=jnp.float32
        )
        normed_two, factor_two = norm_rows(residual, feedforward_gain_f)
        normed_two_low = normed_two.astype(low)
        gate_values = jnp.dot(normed_two_low, gate_weight, preferred_element_type=jnp.float32)
        up_values = jnp.dot(normed_two_low, up_weight, preferred_element_type=jnp.float32)
        sigmoid_gate = jax.nn.sigmoid(gate_values)
        silu_gate = gate_values * sigmoid_gate
        hidden_low = (silu_gate * up_values).astype(low)
        grad_hidden_rows = grad_hidden[first:end]
        grad_gate = (
            grad_hidden_rows * up_values * sigmoid_gate * (1.0 + gate_values * (1.0 - sigmoid_gate))
        ).astype(low)
        grad_up = (grad_hidden_rows * silu_gate).astype(low)
        grad_normed_part = contract(grad_gate, gate_weight, 1, 1) + contract(
            grad_up, up_weight, 1, 1
        )
        down_part = jnp.dot(hidden_low, down_weight, preferred_element_type=jnp.float32)

        def parts_of(values):
            return [
                row_block(values, ((place + slot) % ranks) * share, share) for slot in range(ranks)
            ]

        grad_normed_two = chain_reduce(parts_of(grad_normed_part), ranks)
        own_first = place * share
        own_residual = row_block(residual, own_first, share)
        own_factor = row_block(factor_two, own_first, share)
        own_mixed = row_block(item["mixed"], own_first, share)
        grad_norm, gain_rows = norm_back(
            own_residual, own_factor, feedforward_gain_f, grad_normed_two
        )
        grad_residual = (
            row_block(cotangent[first:end], own_first, share).astype(jnp.float32) + grad_norm
        )
        grad_residual_low = grad_residual.astype(low)
        grad_mixed_own = contract(grad_residual_low, whole_weight, 1, 1)
        pieces = []
        for slot in range(ranks):
            dest = (place + slot) % ranks
            piece = lax.dynamic_slice_in_dim(grad_mixed_own, dest * local_width, local_width, axis=1)
            if slot:
                piece = lax.ppermute(
                    piece, "tensor", [(i, (i + slot) % ranks) for i in range(ranks)]
                )
            pieces.append(piece)
        swapped = jnp.concatenate(pieces[::-1] + pieces[::-1][:-1], axis=0)
        grad_mixed = row_block(swapped, (ranks - 1 - place) * share, rows)
        grad_mixed = (grad_mixed * unit).astype(low)

        down_sum = chain_reduce(parts_of(down_part), ranks)
        block_slots = chain_gather(own_residual + down_sum, ranks, place)
        item.update(
            normed_two=normed_two_low,
            hidden=hidden_low,
            grad_gate=grad_gate,
            grad_up=grad_up,
            gain_rows=jnp.sum(gain_rows, axis=0),
            grad_residual=grad_residual,
            output_grad=(own_mixed, grad_residual_low),
            grad_mixed=grad_mixed,
            block_slots=block_slots,
        )

    def joined(name):
        return jnp.concatenate([item[name] for item in state], axis=0)

    def ordered(slots):
        share = slots[0].shape[0]
        backwards = slots[::-1]
        both = jnp.concatenate(backwards + backwards[:-1], axis=0)
        return row_block(both, (ranks - 1 - place) * share, share * ranks)

    block_output = jnp.concatenate([ordered(item["block_slots"]) for item in state], axis=0)
    block_output = (block_output * unit).astype(low)
    down_grad = contract(joined("hidden"), cotangent, 0, 0)
    down_share = lax.psum_scatter(down_grad, "dp", scatter_dimension=1, tiled=True)
    gate_up_grad = contract(
        joined("normed_two"),
        jnp.concatenate([joined("grad_gate"), joined("grad_up")], axis=1),
        0,
        0,
    )
    gate_up_share = lax.psum_scatter(gate_up_grad, "dp", scatter_dimension=0, tiled=True)
    hidden_width = gate_weight.shape[1]
    gate_share = gate_up_share[:, :hidden_width]
    up_share = gate_up_share[:, hidden_width:]

    output_grad = contract(
        jnp.concatenate([item["output_grad"][0] for item in state], axis=0),
        jnp.concatenate([item["output_grad"][1] for item in state], axis=0),
        0,
        0,
    )
    output_part = lax.psum_scatter(output_grad, "dp", scatter_dimension=1, tiled=True)
    output_share = chain_reduce(
        [
            row_block(output_part, ((place + slot) % ranks) * local_width, local_width)
            for slot in range(ranks)
        ],
        ranks,
    )

    key_back = [None] * len(state)
    value_back = [None] * len(state)
    query_gain_part = 0.0
    key_gain_part = 0.0
    for index in reversed(range(len(state))):
        item = state[index]
        sequence, first, end, key_end = item["stream"]
        rows = end - first
        base = sequence * seq_length
        keys = keys_of(item["stream"])
        grad_query_rot, grad_key_rot, grad_value = attend_back(
            query_all[first:end],
            key_all[keys],
            value_all[keys],
            mask_of(item["stream"]),
            item["log_total"],
            item["grad_mixed"].reshape(rows, kv_heads, group_size, head_size),
            score_scale,
        )
        if first > base:
            split = first - base
            key_back[index - 1] = grad_key_rot[:split]
            value_back[index - 1] = grad_value[:split]
            grad_key_rot = grad_key_rot[split:]
            grad_value = grad_value[split:]
        else:
            grad_key_rot = grad_key_rot + key_back[index]
            grad_value = grad_value + value_back[index]
        rows_slice = slice(first, end)
        grad_query_norm = rotate_back(
            grad_query_rot.reshape(rows, query_heads, head_size),
            cosine[rows_slice],
            sine[rows_slice],
        )
        grad_key_norm = rotate_back(
            grad_key_rot.reshape(rows, kv_heads, head_size), cosine[rows_slice], sine[rows_slice]
        )
        grad_query_raw, query_gain_rows = norm_back(
            query_raw[rows_slice], query_factor[rows_slice], query_gain_f, grad_query_norm
        )
        grad_key_raw, key_gain_rows = norm_back(
            key_unrotated[rows_slice], key_factor[rows_slice], key_gain_f, grad_key_norm
        )
        query_gain_part = query_gain_part + jnp.sum(query_gain_rows, axis=(0, 1))
        key_gain_part = key_gain_part + jnp.sum(key_gain_rows, axis=(0, 1))
        grad_query_low = grad_query_raw.reshape(rows, query_heads * head_size).astype(low)
        grad_key_low = grad_key_raw.reshape(rows, kv_heads * head_size).astype(low)
        grad_value_low = grad_value.reshape(rows, kv_heads * head_size).astype(low)
        grad_input_part = (
            contract(grad_query_low, query_weight, 1, 1)
            + contract(grad_key_low, key_matrix, 1, 1)
            + contract(grad_value_low, value_matrix, 1, 1)
        )
        share = rows // ranks
        grad_normed_one = chain_reduce(
            [
                row_block(grad_input_part, ((place + slot) % ranks) * share, share)
                for slot in range(ranks)
            ],
            ranks,
        )
        own_first = first + place * share
        grad_norm, gain_rows = norm_back(
            row_block(inputs, own_first, share),
            row_block(factor_one, own_first, share),
            attention_gain_f,
            grad_normed_one,
        )
        item["attention_gain_rows"] = jnp.sum(gain_rows, axis=0)
        item["tokens_slots"] = chain_gather(item["grad_residual"] + grad_norm, ranks, place)
        item["grads"] = jnp.concatenate([grad_query_low, grad_key_low, grad_value_low], axis=1)

    tokens_grad = jnp.concatenate([ordered(item["tokens_slots"]) for item in state], axis=0)
    tokens_grad = (tokens_grad * unit).astype(low)
    qkv_grad = contract(normed_low, joined("grads"), 0, 0)
    qkv_share = lax.psum_scatter(qkv_grad, "dp", scatter_dimension=0, tiled=True)
    key_width = kv_heads * head_size
    query_share = qkv_share[:, :local_width]
    key_share = qkv_share[:, local_width : local_width + key_width]
    value_share = qkv_share[:, local_width + key_width :]

    gains = lax.psum(
        jnp.concatenate(
            [
                sum(item["attention_gain_rows"] for item in state),
                sum(item["gain_rows"] for item in state),
                query_gain_part,
                key_gain_part,
            ]
        ),
        ("dp", "tensor"),
    )

    def gain_share(first, size):
        part = size // groups
        return lax.dynamic_slice_in_dim(gains, first + group * part, part, axis=0)

    return (
        block_output,
        tokens_grad,
        gain_share(0, model_width),
        query_share,
        key_share,
        value_share,
        gain_share(2 * model_width, head_size),
        gain_share(2 * model_width + head_size, head_size),
        output_share,
        gain_share(model_width, model_width),
        gate_share,
        up_share,
        down_share,
    )


def solution(mesh):
    return jax.shard_map(
        shards,
        mesh=mesh,
        in_specs=(
            P("dp", None),
            P("dp", None),
            P("dp", None),
            P(),
            P(None, "tensor"),
            P(None, "tensor"),
            P(None, "tensor"),
            P(),
            P(),
            P("tensor", None),
            P(),
            P(None, "tensor"),
            P(None, "tensor"),
            P("tensor", None),
            P("dp", None),
        ),
        out_specs=(
            P("dp", None),
            P("dp", None),
            P("dp"),
            P("dp", "tensor"),
            P("dp", "tensor"),
            P("dp", "tensor"),
            P("dp"),
            P("dp"),
            P("tensor", "dp"),
            P("dp"),
            P("dp", "tensor"),
            P("dp", "tensor"),
            P("tensor", "dp"),
        ),
        check_vma=False,
    )
```

```python
import math

import jax
import jax.numpy as jnp
from jax import lax
from jax.sharding import PartitionSpec as P

SPAN = 256
HALF = 512

epsilon = 1e-06
rope_base = 1000000.0


def contract(left, right, left_dim, right_dim):
    return lax.dot_general(
        left, right, (((left_dim,), (right_dim,)), ((), ())), preferred_element_type=jnp.float32
    )


def norm_rows(values, gain):
    factor = lax.rsqrt(jnp.mean(values * values, axis=-1, keepdims=True) + epsilon)
    return (values * factor * gain, factor)


def norm_back(values, factor, gain, grad_out):
    scaled = grad_out * gain
    inner_sum = jnp.sum(scaled * values, axis=-1, keepdims=True)
    grad_in = factor * scaled - values * (factor * factor * factor) * inner_sum / values.shape[-1]
    return (grad_in, grad_out * values * factor)


def rotate_half(values, cosine, sine):
    half_size = values.shape[-1] // 2
    first_half = values[..., :half_size]
    second_half = values[..., half_size:]
    return jnp.concatenate(
        [first_half * cosine - second_half * sine, second_half * cosine + first_half * sine],
        axis=-1,
    )


def rotate_back(values, cosine, sine):
    half_size = values.shape[-1] // 2
    first_half = values[..., :half_size]
    second_half = values[..., half_size:]
    return jnp.concatenate(
        [first_half * cosine + second_half * sine, second_half * cosine - first_half * sine],
        axis=-1,
    )


def span_mask(starts, seq_length):
    token_index = jnp.arange(seq_length, dtype=jnp.int32)
    inside = (token_index[None, :] >= starts[:, None]) & (
        token_index[None, :] < starts[:, None] + SPAN
    )
    span_number = jnp.arange(starts.shape[0], dtype=jnp.int32)[:, None] + 1
    span_label = jnp.sum(inside.astype(jnp.int32) * span_number, axis=0)
    causal = token_index[:, None] >= token_index[None, :]
    same_span = (span_label[:, None] == span_label[None, :]) & (span_label[:, None] > 0)
    return causal | same_span


def score_block(query_rows, key_heads, allowed, score_scale):
    scores = (
        jnp.einsum("qhgd,khd->hgqk", query_rows, key_heads, preferred_element_type=jnp.float32)
        * score_scale
    )
    return jnp.where(allowed, scores, -jnp.inf)


def attend(query_rows, key_heads, heads_value, allowed, score_scale):
    scores = score_block(query_rows, key_heads, allowed, score_scale)
    highest = jnp.max(scores, axis=-1, keepdims=True)
    exponent = jnp.exp(scores - highest)
    denominator = jnp.sum(exponent, axis=-1, keepdims=True)
    probability = (exponent / denominator).astype(jnp.bfloat16)
    mixed_heads = jnp.einsum(
        "hgqk,khd->qhgd", probability, heads_value, preferred_element_type=jnp.float32
    )
    return (mixed_heads, (highest + jnp.log(denominator))[..., 0])


def attend_back(query_rows, key_heads, heads_value, allowed, log_total, grad_mixed, score_scale):
    scores = score_block(query_rows, key_heads, allowed, score_scale)
    probability = jnp.exp(scores - log_total[..., None])
    grad_value = jnp.einsum(
        "hgqk,qhgd->khd",
        probability.astype(jnp.bfloat16),
        grad_mixed,
        preferred_element_type=jnp.float32,
    )
    grad_prob = jnp.einsum(
        "qhgd,khd->hgqk", grad_mixed, heads_value, preferred_element_type=jnp.float32
    )
    grad_scores = probability * (
        grad_prob - jnp.sum(probability * grad_prob, axis=-1, keepdims=True)
    )
    grad_low = grad_scores.astype(jnp.bfloat16)
    grad_queries = (
        jnp.einsum("hgqk,khd->qhgd", grad_low, key_heads, preferred_element_type=jnp.float32)
        * score_scale
    )
    grad_keys = (
        jnp.einsum("hgqk,qhgd->khd", grad_low, query_rows, preferred_element_type=jnp.float32)
        * score_scale
    )
    return (grad_queries, grad_keys, grad_value)


class Line:
    def __init__(self):
        self.count = lax.axis_size("tensor")
        self.place = lax.axis_index("tensor")
        self.behind = [
            jnp.where(self.place >= slot, self.place - slot, self.place - slot + self.count)
            for slot in range(self.count)
        ]

    def ahead(self, slot):
        return self.behind[(self.count - slot) % self.count]

    def gather_step(self, pair, step):
        count = self.count
        return (
            lax.ppermute(pair[0], "tensor", [(i, i + 1) for i in range(step - 1, count - 1)]),
            lax.ppermute(pair[1], "tensor", [(i, i - 1) for i in range(1, count - step + 1)]),
        )

    def reduce_step(self, pair, step):
        count = self.count
        return (
            lax.ppermute(pair[0], "tensor", [(i, i + 1) for i in range(step)]),
            lax.ppermute(pair[1], "tensor", [(i, i - 1) for i in range(count - step, count)]),
        )

    def slots(self, pairs):
        return [pairs[0][0]] + [
            jnp.where(self.place >= slot, pairs[slot][0], pairs[self.count - slot][1])
            for slot in range(1, self.count)
        ]


class Gather:
    def __init__(self, line, block):
        self.line = line
        self.pairs = [(block, block)]

    def go(self, *after):
        step = len(self.pairs)
        if step < self.line.count:
            pair = tied(self.pairs[-1], *after)
            self.pairs.append(lax.optimization_barrier(self.line.gather_step(pair, step)))

    @property
    def last(self):
        return self.pairs[-1]

    def slots(self):
        while len(self.pairs) < self.line.count:
            self.go()
        return self.line.slots(self.pairs)


class Reduce:
    def __init__(self, line, part):
        self.line = line
        self.part = part
        self.step = 0
        self.last = None

    def go(self, *after):
        count = self.line.count
        if self.step == count - 1:
            return
        pair = (self.part(count - 1 - self.step), self.part((self.step + 1) % count))
        if after:
            pair = tied(pair, *after)
        if self.last is not None:
            pair = (self.last[0] + pair[0], self.last[1] + pair[1])
        self.step += 1
        self.last = lax.optimization_barrier(self.line.reduce_step(pair, self.step))

    def total(self, *after):
        while self.step < self.line.count - 1:
            self.go()
        pair = tied(self.last, *after)
        return self.part(0) + pair[0] + pair[1]


def row_block(values, start, rows):
    return lax.dynamic_slice_in_dim(values, start, rows, axis=0)


def tied(values, *before):
    return lax.optimization_barrier((values, before))[0]


def shards(
    tokens,
    positions,
    span_starts,
    attention_gain,
    query_weight,
    key_matrix,
    value_matrix,
    query_gain,
    key_gain,
    output_weight,
    feedforward_gain,
    gate_weight,
    up_weight,
    down_weight,
    cotangent,
):
    low = jnp.bfloat16
    line = Line()
    ranks = line.count
    place = line.place
    groups = lax.axis_size("dp")
    group = lax.axis_index("dp")
    seq_length = positions.shape[1]
    head_size = query_gain.shape[0]
    model_width, local_width = query_weight.shape
    query_heads = local_width // head_size
    kv_heads = key_matrix.shape[1] // head_size
    group_size = query_heads // kv_heads
    score_scale = head_size ** (-0.5)
    attention_gain_f = attention_gain.astype(jnp.float32)
    feedforward_gain_f = feedforward_gain.astype(jnp.float32)
    query_gain_f = query_gain.astype(jnp.float32)
    key_gain_f = key_gain.astype(jnp.float32)

    unit = jnp.where(positions[0, 0] >= 0, 1.0, 0.0)

    weight_rows = local_width // groups
    own_rows = row_block(output_weight, group * weight_rows, weight_rows).astype(jnp.float32)
    gathered_weight = lax.all_gather(lax.all_gather(own_rows, "tensor", axis=0), "dp", axis=0)

    inputs = tokens.astype(jnp.float32)
    normalized_rows, factor_one = norm_rows(inputs, attention_gain_f)
    normed_low = normalized_rows.astype(low)
    query_raw = jnp.dot(normed_low, query_weight, preferred_element_type=jnp.float32).reshape(
        seq_length, query_heads, head_size
    )
    key_unrotated = jnp.dot(normed_low, key_matrix, preferred_element_type=jnp.float32).reshape(
        seq_length, kv_heads, head_size
    )
    value_low = jnp.dot(normed_low, value_matrix, preferred_element_type=jnp.float32).astype(low)
    frequency = jnp.exp(
        jnp.arange(head_size // 2, dtype=jnp.float32) * (-2.0 * math.log(rope_base) / head_size)
    )
    angles = positions.astype(jnp.float32).reshape(seq_length)[:, None] * frequency
    cosine = jnp.cos(angles)[:, None, :]
    sine = jnp.sin(angles)[:, None, :]
    query_normed, query_factor = norm_rows(query_raw, query_gain_f)
    key_normed, key_factor = norm_rows(key_unrotated, key_gain_f)
    query_low = rotate_half(query_normed, cosine, sine).astype(low)
    key_low = rotate_half(key_normed, cosine, sine).astype(low)
    query_all = query_low.reshape(seq_length, kv_heads, group_size, head_size)
    key_all = key_low.reshape(seq_length, kv_heads, head_size)
    value_all = value_low.reshape(seq_length, kv_heads, head_size)
    mask = span_mask(span_starts[0], seq_length)

    late = slice(HALF, seq_length)
    early = slice(0, HALF)
    seen = {0: slice(0, seq_length), 1: early}
    rows_of = {0: late, 1: early}
    share_of = {0: (seq_length - HALF) // ranks, 1: HALF // ranks}

    def part_of(values, share):
        return lambda slot: row_block(values, line.ahead(slot) * share, share)

    def in_order(slots, buffer=None, first=0):
        share, width = slots[0].shape
        if buffer is None:
            buffer = jnp.zeros((share * ranks, width), low)
        for slot in range(ranks):
            buffer = lax.dynamic_update_slice_in_dim(
                buffer, (slots[slot] * unit).astype(low), first + line.behind[slot] * share, axis=0
            )
        return buffer

    def forward_half(half, query_rows):
        mixed, log_total = attend(
            query_rows,
            key_all[seen[half]],
            value_all[seen[half]],
            mask[rows_of[half], seen[half]],
            score_scale,
        )
        return mixed.reshape(-1, local_width), log_total

    mixed_0, total_0 = forward_half(0, query_all[late])
    heads_0 = Gather(line, mixed_0)
    heads_0.go()
    mixed_1, total_1 = forward_half(1, tied(query_all[early], mixed_0))
    log_total = {0: total_0, 1: total_1}
    gathered_1 = lax.all_gather(mixed_1, "tensor", axis=0)
    first_step = heads_0.last
    heads_0.go()
    grad_hidden = contract(tied(cotangent, mixed_1, first_step), down_weight, 1, 1)
    heads_0.go(grad_hidden)
    gathered_weight = tied(gathered_weight, grad_hidden)
    whole_weight = (
        jnp.concatenate(
            [
                lax.dynamic_slice_in_dim(gathered_weight, line.behind[slot], 1, axis=1).reshape(
                    local_width, model_width
                )
                for slot in range(ranks)
            ],
            axis=0,
        )
        * unit
    ).astype(low)

    def whole_heads(slots):
        return jnp.concatenate([(block * unit).astype(low) for block in slots], axis=1)

    def residual_rows(half, mixed_whole):
        residual = tokens[rows_of[half]].astype(jnp.float32) + jnp.dot(
            mixed_whole, whole_weight, preferred_element_type=jnp.float32
        )
        normed_two, factor_two = norm_rows(residual, feedforward_gain_f)
        return residual, factor_two, normed_two.astype(low)

    def gate_up(normed_two_low):
        return (
            jnp.dot(normed_two_low, gate_weight, preferred_element_type=jnp.float32),
            jnp.dot(normed_two_low, up_weight, preferred_element_type=jnp.float32),
        )

    def feed_forward(half, gate_values, up_values, between=None):
        sigmoid_gate = jax.nn.sigmoid(gate_values)
        silu_gate = gate_values * sigmoid_gate
        hidden_low = (silu_gate * up_values).astype(low)
        grad_hidden_rows = grad_hidden[rows_of[half]]
        grad_gate = (
            grad_hidden_rows * up_values * sigmoid_gate * (1.0 + gate_values * (1.0 - sigmoid_gate))
        ).astype(low)
        grad_up = (grad_hidden_rows * silu_gate).astype(low)
        if between is not None:
            grad_gate, grad_up = tied((grad_gate, grad_up), between(hidden_low))
        grad_normed_part = contract(grad_gate, gate_weight, 1, 1) + contract(
            grad_up, up_weight, 1, 1
        )
        return hidden_low, grad_gate, grad_up, grad_normed_part

    def own_rows_back(half, residual, factor_two, grad_normed_two):
        share = share_of[half]
        own_first = place * share
        own_residual = row_block(residual, own_first, share)
        grad_norm, gain_rows = norm_back(
            own_residual,
            row_block(factor_two, own_first, share),
            feedforward_gain_f,
            grad_normed_two,
        )
        grad_residual = (
            row_block(cotangent[rows_of[half]], own_first, share).astype(jnp.float32) + grad_norm
        )
        grad_residual_low = grad_residual.astype(low)
        grad_mixed_own = contract(grad_residual_low, whole_weight, 1, 1)
        return grad_residual, grad_residual_low, jnp.sum(gain_rows, axis=0), grad_mixed_own

    def swap_heads(grad_mixed_own):
        blocks = []
        for slot in range(ranks):
            first = (ranks - slot) % ranks * local_width
            piece = grad_mixed_own[:, first : first + local_width]
            if slot:
                piece = lax.ppermute(
                    piece, "tensor", [(i, (i + slot) % ranks) for i in range(ranks)]
                )
            blocks.append(piece)
        return in_order(blocks)

    mixed_whole_0 = whole_heads(tied(heads_0.slots(), whole_weight))
    residual_0, factor_0, normed_0 = residual_rows(0, mixed_whole_0)
    gate_0, up_0 = gate_up(normed_0)
    hidden_0, grad_gate_0, grad_up_0, part_0 = feed_forward(0, gate_0, up_0)
    normed_sum_0 = Reduce(line, part_of(part_0, share_of[0]))
    normed_sum_0.go()
    down_part_0 = jnp.dot(tied(hidden_0, part_0), down_weight, preferred_element_type=jnp.float32)

    gathered_1 = tied(gathered_1, down_part_0)
    mixed_whole_1 = whole_heads([row_block(gathered_1, line.behind[slot], 1)[0] for slot in range(ranks)])
    first_step = normed_sum_0.last
    normed_sum_0.go()
    residual_1, factor_1, normed_1 = residual_rows(1, tied(mixed_whole_1, first_step))
    down_sum_0 = Reduce(line, part_of(down_part_0, share_of[0]))
    down_sum_0.go(first_step, normed_1)
    gate_1, up_1 = gate_up(normed_1)
    gate_1, up_1 = tied((gate_1, up_1), normed_sum_0.last)
    normed_sum_0.go()
    down_grads = []

    def all_down_grad(hidden_1):
        hidden = jnp.concatenate([hidden_1, hidden_0], axis=0)
        down_grads.append(contract(hidden, cotangent, 0, 0))
        return down_grads[0], down_sum_0.last

    hidden_1, grad_gate_1, grad_up_1, part_1 = feed_forward(1, gate_1, up_1, all_down_grad)
    down_grad = down_grads[0]
    down_share = lax.psum_scatter(down_grad, "dp", scatter_dimension=1, tiled=True)
    down_sum_0.go(down_grad)
    normed_sum_1 = Reduce(line, part_of(part_1, share_of[1]))
    normed_sum_1.go()

    back_0 = own_rows_back(0, residual_0, factor_0, normed_sum_0.total(part_1))
    grad_mixed_0 = swap_heads(tied(back_0[3], down_sum_0.last))
    down_part_1 = jnp.dot(tied(hidden_1, back_0[3]), down_weight, preferred_element_type=jnp.float32)
    normed_two = jnp.concatenate([normed_1, normed_0], axis=0)
    grad_gate_up = jnp.concatenate(
        [
            jnp.concatenate([grad_gate_1, grad_up_1], axis=1),
            jnp.concatenate([grad_gate_0, grad_up_0], axis=1),
        ],
        axis=0,
    )
    gate_up_grad = contract(tied(normed_two, down_part_1), grad_gate_up, 0, 0)
    hidden_width = gate_weight.shape[1]
    down_sum_1 = Reduce(line, part_of(down_part_1, share_of[1]))

    def attention_core(half, grad_mixed):
        rows = rows_of[half]
        count = rows.stop - rows.start
        return attend_back(
            query_all[rows],
            key_all[seen[half]],
            value_all[seen[half]],
            mask[rows, seen[half]],
            log_total[half],
            grad_mixed.reshape(count, kv_heads, group_size, head_size),
            score_scale,
        )

    def attention_rest(half, core, extra, *before):
        rows = rows_of[half]
        count = rows.stop - rows.start
        grad_query_rot, grad_key_rot, grad_value = core
        if extra is None:
            rest = (grad_key_rot[early], grad_value[early])
            grad_key_rot = grad_key_rot[late]
            grad_value = grad_value[late]
        else:
            rest = None
            grad_key_rot = grad_key_rot + extra[0]
            grad_value = grad_value + extra[1]
        grad_query_norm = rotate_back(
            grad_query_rot.reshape(count, query_heads, head_size), cosine[rows], sine[rows]
        )
        grad_key_norm = rotate_back(
            grad_key_rot.reshape(count, kv_heads, head_size), cosine[rows], sine[rows]
        )
        grad_query_raw, query_gain_rows = norm_back(
            query_raw[rows], query_factor[rows], query_gain_f, grad_query_norm
        )
        grad_key_raw, key_gain_rows = norm_back(
            key_unrotated[rows], key_factor[rows], key_gain_f, grad_key_norm
        )
        gains = (jnp.sum(query_gain_rows, axis=(0, 1)), jnp.sum(key_gain_rows, axis=(0, 1)))
        grad_query_low = grad_query_raw.reshape(count, local_width).astype(low)
        grad_key_low = grad_key_raw.reshape(count, kv_heads * head_size).astype(low)
        grad_value_low = grad_value.reshape(count, kv_heads * head_size).astype(low)
        if before:
            grad_query_low = tied(grad_query_low, *before)
        grad_input_part = (
            contract(grad_query_low, query_weight, 1, 1)
            + contract(grad_key_low, key_matrix, 1, 1)
            + contract(grad_value_low, value_matrix, 1, 1)
        )
        grads = jnp.concatenate([grad_query_low, grad_key_low, grad_value_low], axis=1)
        return rest, gains, grads, grad_input_part

    def tokens_back(half, grad_residual, grad_normed_one):
        share = share_of[half]
        own_first = rows_of[half].start + place * share
        grad_norm, gain_rows = norm_back(
            row_block(tokens, own_first, share).astype(jnp.float32),
            row_block(factor_one, own_first, share),
            attention_gain_f,
            grad_normed_one,
        )
        return grad_residual + grad_norm, jnp.sum(gain_rows, axis=0)

    def own_block(half, residual, down_sum):
        return Gather(
            line, row_block(residual, place * share_of[half], share_of[half]) + down_sum.total()
        )

    first_step = normed_sum_1.last
    normed_sum_1.go(gate_up_grad)
    down_sum_0.go(gate_up_grad)
    core_0 = attention_core(0, tied(grad_mixed_0, gate_up_grad, first_step))
    core_0 = tied(core_0, normed_sum_1.last)
    normed_sum_1.go()
    block_0 = own_block(0, residual_0, down_sum_0)
    block_0.go(core_0)
    rest, gains_0, grads_0, input_part_0 = attention_rest(0, core_0, None)
    input_sum_0 = Reduce(line, part_of(input_part_0, share_of[0]))
    gate_up_share = lax.psum_scatter(
        tied(gate_up_grad, down_share, input_part_0), "dp", scatter_dimension=0, tiled=True
    )
    back_1 = own_rows_back(1, residual_1, factor_1, normed_sum_1.total(input_part_0))
    input_sum_0.go(block_0.last)
    grad_mixed_1 = swap_heads(tied(back_1[3], block_0.last))

    def natural(mixed_whole, half):
        own = row_block(mixed_whole, place * share_of[half], share_of[half])
        return jnp.concatenate(
            [
                lax.dynamic_slice_in_dim(
                    own,
                    jnp.where(place >= rank, place - rank, place - rank + ranks) * local_width,
                    local_width,
                    axis=1,
                )
                for rank in range(ranks)
            ],
            axis=1,
        )

    output_grad = contract(
        jnp.concatenate([natural(mixed_whole_0, 0), natural(mixed_whole_1, 1)], axis=0),
        tied(jnp.concatenate([back_0[1], back_1[1]], axis=0), back_1[3]),
        0,
        0,
    )

    first_step = input_sum_0.last
    input_sum_0.go(output_grad)
    down_sum_1.go(output_grad)
    core_1 = attention_core(1, tied(grad_mixed_1, output_grad, first_step))
    core_1 = tied(core_1, input_sum_0.last)
    input_sum_0.go()
    core_1 = tied(core_1, down_sum_1.last)
    block_0.go(core_1)
    _, gains_1, grads_1, input_part_1 = attention_rest(1, core_1, rest, block_0.last)
    input_sum_1 = Reduce(line, part_of(input_part_1, share_of[1]))
    input_sum_1.go()
    tokens_own_0, attention_gain_0 = tokens_back(0, back_0[0], input_sum_0.total(input_part_1))
    down_sum_1.go(tokens_own_0)
    qkv_grad = contract(
        tied(normed_low, input_part_1, tokens_own_0),
        jnp.concatenate([grads_1, grads_0], axis=0),
        0,
        0,
    )
    key_width = kv_heads * head_size
    output_part = lax.psum_scatter(
        tied(output_grad, gate_up_share, tokens_own_0), "dp", scatter_dimension=1, tiled=True
    )
    output_share = lax.psum_scatter(output_part, "tensor", scatter_dimension=0, tiled=True)

    tokens_0 = Gather(line, tied(tokens_own_0, input_sum_1.last))
    input_sum_1.go(qkv_grad)
    tokens_0.go(qkv_grad)
    before = (input_sum_1.last, down_sum_1.last)
    input_sum_1.go(*before)
    before = (tokens_0.last,)
    tokens_0.go(*before)
    before = (input_sum_1.last,)
    down_sum_1.go(*before)
    tokens_own_1, attention_gain_1 = tokens_back(1, back_1[0], input_sum_1.total(*before))
    tokens_1 = Gather(line, tied(tokens_own_1, tokens_0.last))
    tokens_1.go()
    block_1 = own_block(1, residual_1, down_sum_1)
    tokens_0.go(tokens_1.last, block_1.last)
    block_1.go(tokens_1.last)
    before = (block_1.last, tokens_0.last)
    tokens_1.go(*before)
    block_0.go(*before)
    before = (tokens_1.last, block_0.last)
    tokens_1.go(*before)
    block_1.go(*before)
    block_1.go()
    qkv_share = lax.psum_scatter(
        tied(qkv_grad, output_part, block_1.pairs[1]), "dp", scatter_dimension=0, tiled=True
    )

    tokens_grad = jnp.zeros((seq_length, model_width), low)
    tokens_grad = in_order(tokens_0.slots(), tokens_grad, HALF)
    tokens_grad = in_order(tokens_1.slots(), tokens_grad, 0)
    block_output = jnp.zeros((seq_length, model_width), low)
    block_output = in_order(block_0.slots(), block_output, HALF)
    block_output = in_order(block_1.slots(), block_output, 0)

    gains = lax.psum(
        jnp.concatenate(
            [
                attention_gain_0 + attention_gain_1,
                back_0[2] + back_1[2],
                gains_0[0] + gains_1[0],
                gains_0[1] + gains_1[1],
            ]
        ),
        ("dp", "tensor"),
    )

    def gain_share(first, size):
        part = size // groups
        return lax.dynamic_slice_in_dim(gains, first + group * part, part, axis=0)

    return (
        block_output,
        tokens_grad,
        gain_share(0, model_width),
        qkv_share[:, :local_width],
        qkv_share[:, local_width : local_width + key_width],
        qkv_share[:, local_width + key_width :],
        gain_share(2 * model_width, head_size),
        gain_share(2 * model_width + head_size, head_size),
        output_share,
        gain_share(model_width, model_width),
        gate_up_share[:, :hidden_width],
        gate_up_share[:, hidden_width:],
        down_share,
    )


def solution(mesh):
    return jax.shard_map(
        shards,
        mesh=mesh,
        in_specs=(
            P("dp", None),
            P("dp", None),
            P("dp", None),
            P(),
            P(None, "tensor"),
            P(None, "tensor"),
            P(None, "tensor"),
            P(),
            P(),
            P("tensor", None),
            P(),
            P(None, "tensor"),
            P(None, "tensor"),
            P("tensor", None),
            P("dp", None),
        ),
        out_specs=(
            P("dp", None),
            P("dp", None),
            P("dp"),
            P("dp", "tensor"),
            P("dp", "tensor"),
            P("dp", "tensor"),
            P("dp"),
            P("dp"),
            P("tensor", "dp"),
            P("dp"),
            P("dp", "tensor"),
            P("dp", "tensor"),
            P("tensor", "dp"),
        ),
        check_vma=False,
    )
```

```python
import math

import jax
import jax.numpy as jnp
from jax import lax
from jax.sharding import PartitionSpec as P

SPAN = 256
HALF = 512

epsilon = 1e-06
rope_base = 1000000.0


def contract(left, right, left_dim, right_dim):
    return lax.dot_general(
        left, right, (((left_dim,), (right_dim,)), ((), ())), preferred_element_type=jnp.float32
    )


def norm_rows(values, gain):
    factor = lax.rsqrt(jnp.mean(values * values, axis=-1, keepdims=True) + epsilon)
    return (values * factor * gain, factor)


def norm_back(values, factor, gain, grad_out):
    scaled = grad_out * gain
    inner_sum = jnp.sum(scaled * values, axis=-1, keepdims=True)
    grad_in = factor * scaled - values * (factor * factor * factor) * inner_sum / values.shape[-1]
    return (grad_in, grad_out * values * factor)


def rotate_half(values, cosine, sine):
    half_size = values.shape[-1] // 2
    first_half = values[..., :half_size]
    second_half = values[..., half_size:]
    return jnp.concatenate(
        [first_half * cosine - second_half * sine, second_half * cosine + first_half * sine],
        axis=-1,
    )


def rotate_back(values, cosine, sine):
    half_size = values.shape[-1] // 2
    first_half = values[..., :half_size]
    second_half = values[..., half_size:]
    return jnp.concatenate(
        [first_half * cosine + second_half * sine, second_half * cosine - first_half * sine],
        axis=-1,
    )


def span_mask(starts, seq_length):
    token_index = jnp.arange(seq_length, dtype=jnp.int32)
    inside = (token_index[None, :] >= starts[:, None]) & (
        token_index[None, :] < starts[:, None] + SPAN
    )
    span_number = jnp.arange(starts.shape[0], dtype=jnp.int32)[:, None] + 1
    span_label = jnp.sum(inside.astype(jnp.int32) * span_number, axis=0)
    causal = token_index[:, None] >= token_index[None, :]
    same_span = (span_label[:, None] == span_label[None, :]) & (span_label[:, None] > 0)
    return causal | same_span


def score_block(query_rows, key_heads, allowed, score_scale):
    scores = (
        jnp.einsum("qhgd,khd->hgqk", query_rows, key_heads, preferred_element_type=jnp.float32)
        * score_scale
    )
    return jnp.where(allowed, scores, -jnp.inf)


def attend(query_rows, key_heads, heads_value, allowed, score_scale):
    scores = score_block(query_rows, key_heads, allowed, score_scale)
    highest = jnp.max(scores, axis=-1, keepdims=True)
    exponent = jnp.exp(scores - highest)
    denominator = jnp.sum(exponent, axis=-1, keepdims=True)
    probability = (exponent / denominator).astype(jnp.bfloat16)
    mixed_heads = jnp.einsum(
        "hgqk,khd->qhgd", probability, heads_value, preferred_element_type=jnp.float32
    )
    return (mixed_heads, (highest + jnp.log(denominator))[..., 0])


def attend_back(query_rows, key_heads, heads_value, allowed, log_total, grad_mixed, score_scale):
    scores = score_block(query_rows, key_heads, allowed, score_scale)
    probability = jnp.exp(scores - log_total[..., None])
    grad_value = jnp.einsum(
        "hgqk,qhgd->khd",
        probability.astype(jnp.bfloat16),
        grad_mixed,
        preferred_element_type=jnp.float32,
    )
    grad_prob = jnp.einsum(
        "qhgd,khd->hgqk", grad_mixed, heads_value, preferred_element_type=jnp.float32
    )
    grad_scores = probability * (
        grad_prob - jnp.sum(probability * grad_prob, axis=-1, keepdims=True)
    )
    grad_low = grad_scores.astype(jnp.bfloat16)
    grad_queries = (
        jnp.einsum("hgqk,khd->qhgd", grad_low, key_heads, preferred_element_type=jnp.float32)
        * score_scale
    )
    grad_keys = (
        jnp.einsum("hgqk,qhgd->khd", grad_low, query_rows, preferred_element_type=jnp.float32)
        * score_scale
    )
    return (grad_queries, grad_keys, grad_value)


class Line:
    def __init__(self):
        self.count = lax.axis_size("tensor")
        self.place = lax.axis_index("tensor")
        self.behind = [
            jnp.where(self.place >= slot, self.place - slot, self.place - slot + self.count)
            for slot in range(self.count)
        ]

    def ahead(self, slot):
        return self.behind[(self.count - slot) % self.count]

    def gather_step(self, pair, step):
        count = self.count
        return (
            lax.ppermute(pair[0], "tensor", [(i, i + 1) for i in range(step - 1, count - 1)]),
            lax.ppermute(pair[1], "tensor", [(i, i - 1) for i in range(1, count - step + 1)]),
        )

    def reduce_step(self, pair, step):
        count = self.count
        return (
            lax.ppermute(pair[0], "tensor", [(i, i + 1) for i in range(step)]),
            lax.ppermute(pair[1], "tensor", [(i, i - 1) for i in range(count - step, count)]),
        )

    def slots(self, pairs):
        return [pairs[0][0]] + [
            jnp.where(self.place >= slot, pairs[slot][0], pairs[self.count - slot][1])
            for slot in range(1, self.count)
        ]


class Gather:
    def __init__(self, line, block, name):
        self.line = line
        self.name = name
        self.pairs = [(block, block)]

    def go(self, *after):
        step = len(self.pairs)
        if step < self.line.count:
            pair = tied(self.pairs[-1], *after)
            with jax.named_scope(f"{self.name}_gather_{step}"):
                moved = self.line.gather_step(pair, step)
            self.pairs.append(lax.optimization_barrier(moved))

    @property
    def last(self):
        return self.pairs[-1]

    def slots(self):
        while len(self.pairs) < self.line.count:
            self.go()
        return self.line.slots(self.pairs)


class Reduce:
    def __init__(self, line, part, name):
        self.line = line
        self.name = name
        self.part = part
        self.step = 0
        self.last = None
        self.sent = None

    def go(self, *after):
        count = self.line.count
        if self.step == count - 1:
            return
        pair = (self.part(count - 1 - self.step), self.part((self.step + 1) % count))
        if after:
            pair = tied(pair, *after)
        if self.last is not None:
            pair = (self.last[0] + pair[0], self.last[1] + pair[1])
        self.step += 1
        self.sent = pair = lax.optimization_barrier(pair)
        with jax.named_scope(f"{self.name}_sum_{self.step}"):
            moved = self.line.reduce_step(pair, self.step)
        self.last = lax.optimization_barrier(moved)

    def total(self, *after):
        while self.step < self.line.count - 1:
            self.go()
        pair = tied(self.last, *after)
        return self.part(0) + pair[0] + pair[1]


def row_block(values, start, rows):
    return lax.dynamic_slice_in_dim(values, start, rows, axis=0)


def tied(values, *before):
    return lax.optimization_barrier((values, before))[0]


def shards(
    tokens,
    positions,
    span_starts,
    attention_gain,
    query_weight,
    key_matrix,
    value_matrix,
    query_gain,
    key_gain,
    output_weight,
    feedforward_gain,
    gate_weight,
    up_weight,
    down_weight,
    cotangent,
):
    low = jnp.bfloat16
    line = Line()
    ranks = line.count
    place = line.place
    groups = lax.axis_size("dp")
    group = lax.axis_index("dp")
    seq_length = positions.shape[1]
    head_size = query_gain.shape[0]
    model_width, local_width = query_weight.shape
    query_heads = local_width // head_size
    kv_heads = key_matrix.shape[1] // head_size
    group_size = query_heads // kv_heads
    score_scale = head_size ** (-0.5)
    attention_gain_f = attention_gain.astype(jnp.float32)
    feedforward_gain_f = feedforward_gain.astype(jnp.float32)
    query_gain_f = query_gain.astype(jnp.float32)
    key_gain_f = key_gain.astype(jnp.float32)

    unit = jnp.where(positions[0, 0] >= 0, 1.0, 0.0)

    weight_rows = local_width // groups
    own_rows = row_block(output_weight, group * weight_rows, weight_rows).astype(jnp.float32)
    weight_by_rank = lax.all_gather(own_rows, "tensor", axis=0)

    inputs = tokens.astype(jnp.float32)
    normalized_rows, factor_one = norm_rows(inputs, attention_gain_f)
    normed_low = normalized_rows.astype(low)
    query_raw = jnp.dot(normed_low, query_weight, preferred_element_type=jnp.float32).reshape(
        seq_length, query_heads, head_size
    )
    key_unrotated = jnp.dot(normed_low, key_matrix, preferred_element_type=jnp.float32).reshape(
        seq_length, kv_heads, head_size
    )
    value_low = jnp.dot(normed_low, value_matrix, preferred_element_type=jnp.float32).astype(low)
    frequency = jnp.exp(
        jnp.arange(head_size // 2, dtype=jnp.float32) * (-2.0 * math.log(rope_base) / head_size)
    )
    angles = positions.astype(jnp.float32).reshape(seq_length)[:, None] * frequency
    cosine = jnp.cos(angles)[:, None, :]
    sine = jnp.sin(angles)[:, None, :]
    query_normed, query_factor = norm_rows(query_raw, query_gain_f)
    key_normed, key_factor = norm_rows(key_unrotated, key_gain_f)
    query_low = rotate_half(query_normed, cosine, sine).astype(low)
    key_low = rotate_half(key_normed, cosine, sine).astype(low)
    query_all = query_low.reshape(seq_length, kv_heads, group_size, head_size)
    key_all = key_low.reshape(seq_length, kv_heads, head_size)
    value_all = value_low.reshape(seq_length, kv_heads, head_size)
    mask = span_mask(span_starts[0], seq_length)

    late = slice(HALF, seq_length)
    early = slice(0, HALF)
    seen = {0: slice(0, seq_length), 1: early}
    rows_of = {0: late, 1: early}
    share_of = {0: (seq_length - HALF) // ranks, 1: HALF // ranks}

    def part_of(values, share):
        return lambda slot: row_block(values, line.ahead(slot) * share, share)

    def in_order(slots, buffer=None, first=0):
        share, width = slots[0].shape
        if buffer is None:
            buffer = jnp.zeros((share * ranks, width), low)
        for slot in range(ranks):
            buffer = lax.dynamic_update_slice_in_dim(
                buffer, (slots[slot] * unit).astype(low), first + line.behind[slot] * share, axis=0
            )
        return buffer

    def forward_half(half, query_rows):
        mixed, log_total = attend(
            query_rows,
            key_all[seen[half]],
            value_all[seen[half]],
            mask[rows_of[half], seen[half]],
            score_scale,
        )
        return mixed.reshape(-1, local_width), log_total

    mixed_0, total_0 = forward_half(0, query_all[late])
    heads_0 = Gather(line, mixed_0, "heads_0")
    heads_0.go()
    mixed_1, total_1 = forward_half(1, tied(query_all[early], mixed_0))
    log_total = {0: total_0, 1: total_1}
    heads_1 = Gather(line, mixed_1, "heads_1")
    other_rows = jnp.concatenate(
        [row_block(tied(weight_by_rank, mixed_1), line.behind[slot], 1) for slot in range(1, ranks)]
    )
    gathered_weight = lax.all_gather(other_rows, "dp", axis=0)
    first_step = heads_0.last
    heads_0.go()
    grad_hidden = contract(tied(cotangent, mixed_1, first_step), down_weight, 1, 1)
    second_step = heads_0.last
    heads_0.go(grad_hidden)
    gathered_weight = tied(gathered_weight, grad_hidden)
    whole_weight = jnp.concatenate(
        [output_weight]
        + [
            (gathered_weight[:, slot - 1].reshape(local_width, model_width) * unit).astype(low)
            for slot in range(1, ranks)
        ],
        axis=0,
    )
    heads_1.go(second_step, whole_weight)
    heads_1.go(heads_0.last)

    def whole_heads(slots):
        return jnp.concatenate([(block * unit).astype(low) for block in slots], axis=1)

    def residual_rows(half, mixed_whole):
        residual = tokens[rows_of[half]].astype(jnp.float32) + jnp.dot(
            mixed_whole, whole_weight, preferred_element_type=jnp.float32
        )
        normed_two, factor_two = norm_rows(residual, feedforward_gain_f)
        return residual, factor_two, normed_two.astype(low)

    def gate_up(normed_two_low):
        return (
            jnp.dot(normed_two_low, gate_weight, preferred_element_type=jnp.float32),
            jnp.dot(normed_two_low, up_weight, preferred_element_type=jnp.float32),
        )

    def feed_forward(half, gate_values, up_values, between=None):
        sigmoid_gate = jax.nn.sigmoid(gate_values)
        silu_gate = gate_values * sigmoid_gate
        hidden_low = (silu_gate * up_values).astype(low)
        grad_hidden_rows = grad_hidden[rows_of[half]]
        grad_gate = (
            grad_hidden_rows * up_values * sigmoid_gate * (1.0 + gate_values * (1.0 - sigmoid_gate))
        ).astype(low)
        grad_up = (grad_hidden_rows * silu_gate).astype(low)
        if between is not None:
            grad_gate, grad_up = tied((grad_gate, grad_up), between(hidden_low))
        grad_normed_part = contract(grad_gate, gate_weight, 1, 1) + contract(
            grad_up, up_weight, 1, 1
        )
        return hidden_low, grad_gate, grad_up, grad_normed_part

    def own_rows_back(half, residual, factor_two, grad_normed_two):
        share = share_of[half]
        own_first = place * share
        own_residual = row_block(residual, own_first, share)
        grad_norm, gain_rows = norm_back(
            own_residual,
            row_block(factor_two, own_first, share),
            feedforward_gain_f,
            grad_normed_two,
        )
        grad_residual = (
            row_block(cotangent[rows_of[half]], own_first, share).astype(jnp.float32) + grad_norm
        )
        grad_residual_low = grad_residual.astype(low)
        grad_mixed_own = contract(grad_residual_low, whole_weight, 1, 1)
        return grad_residual, grad_residual_low, jnp.sum(gain_rows, axis=0), grad_mixed_own

    def swap_heads(grad_mixed_own, *before):
        blocks = []
        for slot in range(ranks):
            first = (ranks - slot) % ranks * local_width
            piece = grad_mixed_own[:, first : first + local_width]
            if slot:
                piece = lax.ppermute(
                    piece, "tensor", [(i, (i + slot) % ranks) for i in range(ranks)]
                )
            blocks.append(piece)
        return in_order(tied(blocks, *before))

    mixed_whole_0 = whole_heads(tied(heads_0.slots(), whole_weight))
    residual_0, factor_0, normed_0 = residual_rows(0, mixed_whole_0)
    gate_0, up_0 = gate_up(normed_0)
    heads_1.go(gate_0)
    hidden_0, grad_gate_0, grad_up_0, part_0 = feed_forward(0, gate_0, up_0)
    normed_sum_0 = Reduce(line, part_of(part_0, share_of[0]), "normed_0")
    normed_sum_0.go()
    down_part_0 = jnp.dot(tied(hidden_0, part_0), down_weight, preferred_element_type=jnp.float32)

    mixed_whole_1 = whole_heads(tied(heads_1.slots(), down_part_0))
    normed_sum_0.go(down_part_0)
    mixed_whole_1 = tied(mixed_whole_1, normed_sum_0.last)
    normed_sum_0.go()
    residual_1, factor_1, normed_1 = residual_rows(1, tied(mixed_whole_1, normed_sum_0.sent))
    gate_1, up_1 = gate_up(normed_1)
    down_sum_0 = Reduce(line, part_of(down_part_0, share_of[0]), "down_0")
    stages = []

    def late_sums(hidden_1):
        hidden = jnp.concatenate([hidden_1, hidden_0], axis=0)
        down_grad = contract(hidden, cotangent, 0, 0)
        down_sum_0.go(normed_sum_0.last)
        back = own_rows_back(0, residual_0, factor_0, normed_sum_0.total(down_sum_0.sent))
        stages.extend([down_grad, back])
        return down_grad, back[3], down_sum_0.last

    hidden_1, grad_gate_1, grad_up_1, part_1 = feed_forward(1, gate_1, up_1, late_sums)
    down_grad, back_0 = stages
    down_share = lax.psum_scatter(
        tied(down_grad, down_sum_0.last), "dp", scatter_dimension=1, tiled=True
    )
    down_sum_0.go()
    normed_sum_1 = Reduce(line, part_of(part_1, share_of[1]), "normed_1")
    down_part_1 = jnp.dot(tied(hidden_1, part_1), down_weight, preferred_element_type=jnp.float32)
    grad_mixed_0 = swap_heads(back_0[3], down_part_1)
    down_sum_0.go(grad_mixed_0)
    normed_two = jnp.concatenate([normed_1, normed_0], axis=0)
    grad_gate_up = jnp.concatenate(
        [
            jnp.concatenate([grad_gate_1, grad_up_1], axis=1),
            jnp.concatenate([grad_gate_0, grad_up_0], axis=1),
        ],
        axis=0,
    )
    gate_up_grad = contract(tied(normed_two, down_sum_0.sent), grad_gate_up, 0, 0)
    hidden_width = gate_weight.shape[1]
    down_sum_1 = Reduce(line, part_of(down_part_1, share_of[1]), "down_1")

    def attention_core(half, grad_mixed):
        rows = rows_of[half]
        count = rows.stop - rows.start
        return attend_back(
            query_all[rows],
            key_all[seen[half]],
            value_all[seen[half]],
            mask[rows, seen[half]],
            log_total[half],
            grad_mixed.reshape(count, kv_heads, group_size, head_size),
            score_scale,
        )

    def attention_rest(half, core, extra, *before):
        rows = rows_of[half]
        count = rows.stop - rows.start
        grad_query_rot, grad_key_rot, grad_value = core
        if extra is None:
            rest = (grad_key_rot[early], grad_value[early])
            grad_key_rot = grad_key_rot[late]
            grad_value = grad_value[late]
        else:
            rest = None
            grad_key_rot = grad_key_rot + extra[0]
            grad_value = grad_value + extra[1]
        grad_query_norm = rotate_back(
            grad_query_rot.reshape(count, query_heads, head_size), cosine[rows], sine[rows]
        )
        grad_key_norm = rotate_back(
            grad_key_rot.reshape(count, kv_heads, head_size), cosine[rows], sine[rows]
        )
        grad_query_raw, query_gain_rows = norm_back(
            query_raw[rows], query_factor[rows], query_gain_f, grad_query_norm
        )
        grad_key_raw, key_gain_rows = norm_back(
            key_unrotated[rows], key_factor[rows], key_gain_f, grad_key_norm
        )
        gains = (jnp.sum(query_gain_rows, axis=(0, 1)), jnp.sum(key_gain_rows, axis=(0, 1)))
        grad_query_low = grad_query_raw.reshape(count, local_width).astype(low)
        grad_key_low = grad_key_raw.reshape(count, kv_heads * head_size).astype(low)
        grad_value_low = grad_value.reshape(count, kv_heads * head_size).astype(low)
        if before:
            grad_query_low = tied(grad_query_low, *before)
        grad_input_part = (
            contract(grad_query_low, query_weight, 1, 1)
            + contract(grad_key_low, key_matrix, 1, 1)
            + contract(grad_value_low, value_matrix, 1, 1)
        )
        grads = jnp.concatenate([grad_query_low, grad_key_low, grad_value_low], axis=1)
        return rest, gains, grads, grad_input_part

    def tokens_back(half, grad_residual, grad_normed_one):
        share = share_of[half]
        own_first = rows_of[half].start + place * share
        grad_norm, gain_rows = norm_back(
            row_block(tokens, own_first, share).astype(jnp.float32),
            row_block(factor_one, own_first, share),
            attention_gain_f,
            grad_normed_one,
        )
        return grad_residual + grad_norm, jnp.sum(gain_rows, axis=0)

    def own_block(half, residual, down_sum):
        return Gather(
            line,
            row_block(residual, place * share_of[half], share_of[half]) + down_sum.total(),
            f"block_{half}",
        )

    block_0 = own_block(0, residual_0, down_sum_0)
    block_0.go()
    gate_up_share = lax.psum_scatter(
        tied(gate_up_grad, down_share, block_0.last), "dp", scatter_dimension=0, tiled=True
    )
    before = (block_0.last,)
    normed_sum_1.go(*before)
    block_0.go(*before)
    core_0 = attention_core(0, tied(grad_mixed_0, gate_up_grad, normed_sum_1.sent))
    before = (normed_sum_1.last, block_0.last)
    normed_sum_1.go(*before)
    block_0.go(*before)
    rest, gains_0, grads_0, input_part_0 = attention_rest(
        0, tied(core_0, normed_sum_1.sent), None
    )
    input_sum_0 = Reduce(line, part_of(input_part_0, share_of[0]), "input_0")
    before = (normed_sum_1.last, block_0.last)
    normed_sum_1.go(*before)
    back_1 = own_rows_back(1, residual_1, factor_1, normed_sum_1.total())
    grad_mixed_1 = swap_heads(back_1[3])
    input_sum_0.go(back_1[3])

    def natural(mixed_whole, half):
        own = row_block(mixed_whole, place * share_of[half], share_of[half])
        return jnp.concatenate(
            [
                lax.dynamic_slice_in_dim(
                    own,
                    jnp.where(place >= rank, place - rank, place - rank + ranks) * local_width,
                    local_width,
                    axis=1,
                )
                for rank in range(ranks)
            ],
            axis=1,
        )

    output_grad = contract(
        jnp.concatenate([natural(mixed_whole_0, 0), natural(mixed_whole_1, 1)], axis=0),
        tied(jnp.concatenate([back_0[1], back_1[1]], axis=0), back_1[3]),
        0,
        0,
    )

    output_part = lax.psum_scatter(
        tied(output_grad, gate_up_share, input_sum_0.last, grad_mixed_1),
        "dp",
        scatter_dimension=1,
        tiled=True,
    )
    input_sum_0.go(grad_mixed_1)
    core_1 = attention_core(1, tied(grad_mixed_1, input_sum_0.sent))
    _, gains_1, grads_1, input_part_1 = attention_rest(1, core_1, rest)
    input_sum_1 = Reduce(line, part_of(input_part_1, share_of[1]), "input_1")
    tokens_own_0, attention_gain_0 = tokens_back(0, back_0[0], input_sum_0.total())
    tokens_0 = Gather(line, tokens_own_0, "tokens_0")
    tokens_0.go()
    qkv_grad = contract(
        tied(normed_low, tokens_own_0),
        jnp.concatenate([grads_1, grads_0], axis=0),
        0,
        0,
    )
    key_width = kv_heads * head_size

    before = (tokens_0.last,)
    down_sum_1.go(*before)
    tokens_0.go(*before)
    before = (tokens_0.last, down_sum_1.last)
    down_sum_1.go(*before)
    tokens_0.go(*before)
    before = (tokens_0.last, down_sum_1.last)
    down_sum_1.go(*before)
    qkv_share = lax.psum_scatter(
        tied(qkv_grad, output_part, down_sum_1.last), "dp", scatter_dimension=0, tiled=True
    )
    block_1 = own_block(1, residual_1, down_sum_1)
    block_1.go()
    before = (block_1.last,)
    input_sum_1.go(*before)
    block_1.go(*before)
    before = (input_sum_1.last, block_1.last)
    input_sum_1.go(*before)
    block_1.go(*before)
    before = (input_sum_1.last, block_1.last)
    input_sum_1.go(*before)
    tokens_own_1, attention_gain_1 = tokens_back(1, back_1[0], input_sum_1.total())
    tokens_1 = Gather(line, tokens_own_1, "tokens_1")
    gains = jnp.concatenate(
        [
            attention_gain_0 + attention_gain_1,
            back_0[2] + back_1[2],
            gains_0[0] + gains_1[0],
            gains_0[1] + gains_1[1],
        ]
    )

    exchanges = [("dp", groups, 1 << bit) for bit in range((groups - 1).bit_length())]
    exchanges += [("tensor", ranks, 1 << bit) for bit in range((ranks - 1).bit_length())]
    output_sum = Reduce(line, part_of(output_part, local_width), "output")
    while len(tokens_1.pairs) < ranks or exchanges:
        tokens_1.go()
        if len(tokens_1.pairs) > 2:
            output_sum.go(tokens_1.pairs[-2])
            tokens_1.pairs[-1], output_sum.last = lax.optimization_barrier(
                (tokens_1.last, output_sum.last)
            )
        for axis, size, distance in exchanges[:2]:
            gains = gains + lax.ppermute(gains, axis, [(i, i ^ distance) for i in range(size)])
        exchanges = exchanges[2:]
        tokens_1.pairs[-1], gains = lax.optimization_barrier((tokens_1.last, gains))

    tokens_grad = jnp.zeros((seq_length, model_width), low)
    tokens_grad = in_order(tokens_0.slots(), tokens_grad, HALF)
    block_output = jnp.zeros((seq_length, model_width), low)
    block_output = in_order(block_0.slots(), block_output, HALF)
    block_output = in_order(block_1.slots(), block_output, 0)
    shares = (
        qkv_share[:, :local_width],
        qkv_share[:, local_width : local_width + key_width],
        qkv_share[:, local_width + key_width :],
        gate_up_share[:, :hidden_width],
        gate_up_share[:, hidden_width:],
    )
    output_sum.go()
    output_share = output_sum.total(shares, block_output)
    last_slots = tokens_1.slots()
    tokens_grad = in_order(last_slots, tokens_grad, 0)

    def gain_share(first, size):
        part = size // groups
        return lax.dynamic_slice_in_dim(gains, first + group * part, part, axis=0)

    return (
        block_output,
        tokens_grad,
        gain_share(0, model_width),
        shares[0],
        shares[1],
        shares[2],
        gain_share(2 * model_width, head_size),
        gain_share(2 * model_width + head_size, head_size),
        output_share,
        gain_share(model_width, model_width),
        shares[3],
        shares[4],
        down_share,
    )


def solution(mesh):
    return jax.shard_map(
        shards,
        mesh=mesh,
        in_specs=(
            P("dp", None),
            P("dp", None),
            P("dp", None),
            P(),
            P(None, "tensor"),
            P(None, "tensor"),
            P(None, "tensor"),
            P(),
            P(),
            P("tensor", None),
            P(),
            P(None, "tensor"),
            P(None, "tensor"),
            P("tensor", None),
            P("dp", None),
        ),
        out_specs=(
            P("dp", None),
            P("dp", None),
            P("dp"),
            P("dp", "tensor"),
            P("dp", "tensor"),
            P("dp", "tensor"),
            P("dp"),
            P("dp"),
            P("tensor", "dp"),
            P("dp"),
            P("dp", "tensor"),
            P("dp", "tensor"),
            P("tensor", "dp"),
        ),
        check_vma=False,
    )
```

```python
import math

import jax
import jax.numpy as jnp
from jax import lax
from jax.sharding import PartitionSpec as P

SPAN = 256
HALF = 512

epsilon = 1e-06
rope_base = 1000000.0


def contract(left, right, left_dim, right_dim):
    return lax.dot_general(
        left, right, (((left_dim,), (right_dim,)), ((), ())), preferred_element_type=jnp.float32
    )


def norm_rows(values, gain):
    factor = lax.rsqrt(jnp.mean(values * values, axis=-1, keepdims=True) + epsilon)
    return (values * factor * gain, factor)


def norm_back(values, factor, gain, grad_out):
    scaled = grad_out * gain
    inner_sum = jnp.sum(scaled * values, axis=-1, keepdims=True)
    grad_in = factor * scaled - values * (factor * factor * factor) * inner_sum / values.shape[-1]
    return (grad_in, grad_out * values * factor)


def rotate_half(values, cosine, sine):
    half_size = values.shape[-1] // 2
    first_half = values[..., :half_size]
    second_half = values[..., half_size:]
    return jnp.concatenate(
        [first_half * cosine - second_half * sine, second_half * cosine + first_half * sine],
        axis=-1,
    )


def rotate_back(values, cosine, sine):
    half_size = values.shape[-1] // 2
    first_half = values[..., :half_size]
    second_half = values[..., half_size:]
    return jnp.concatenate(
        [first_half * cosine + second_half * sine, second_half * cosine - first_half * sine],
        axis=-1,
    )


def span_mask(starts, seq_length):
    token_index = jnp.arange(seq_length, dtype=jnp.int32)
    inside = (token_index[None, :] >= starts[:, None]) & (
        token_index[None, :] < starts[:, None] + SPAN
    )
    span_number = jnp.arange(starts.shape[0], dtype=jnp.int32)[:, None] + 1
    span_label = jnp.sum(inside.astype(jnp.int32) * span_number, axis=0)
    causal = token_index[:, None] >= token_index[None, :]
    same_span = (span_label[:, None] == span_label[None, :]) & (span_label[:, None] > 0)
    return causal | same_span


def score_block(query_rows, key_heads, allowed, score_scale):
    scores = (
        jnp.einsum("qhgd,khd->hgqk", query_rows, key_heads, preferred_element_type=jnp.float32)
        * score_scale
    )
    return jnp.where(allowed, scores, -jnp.inf)


def attend(query_rows, key_heads, heads_value, allowed, score_scale):
    scores = score_block(query_rows, key_heads, allowed, score_scale)
    highest = jnp.max(scores, axis=-1, keepdims=True)
    exponent = jnp.exp(scores - highest)
    denominator = jnp.sum(exponent, axis=-1, keepdims=True)
    probability = (exponent / denominator).astype(jnp.bfloat16)
    mixed_heads = jnp.einsum(
        "hgqk,khd->qhgd", probability, heads_value, preferred_element_type=jnp.float32
    )
    return (mixed_heads, (highest + jnp.log(denominator))[..., 0])


def attend_back(query_rows, key_heads, heads_value, allowed, log_total, grad_mixed, score_scale):
    scores = score_block(query_rows, key_heads, allowed, score_scale)
    probability = jnp.exp(scores - log_total[..., None])
    grad_value = jnp.einsum(
        "hgqk,qhgd->khd",
        probability.astype(jnp.bfloat16),
        grad_mixed,
        preferred_element_type=jnp.float32,
    )
    grad_prob = jnp.einsum(
        "qhgd,khd->hgqk", grad_mixed, heads_value, preferred_element_type=jnp.float32
    )
    grad_scores = probability * (
        grad_prob - jnp.sum(probability * grad_prob, axis=-1, keepdims=True)
    )
    grad_low = grad_scores.astype(jnp.bfloat16)
    grad_queries = (
        jnp.einsum("hgqk,khd->qhgd", grad_low, key_heads, preferred_element_type=jnp.float32)
        * score_scale
    )
    grad_keys = (
        jnp.einsum("hgqk,qhgd->khd", grad_low, query_rows, preferred_element_type=jnp.float32)
        * score_scale
    )
    return (grad_queries, grad_keys, grad_value)


class Line:
    def __init__(self):
        self.count = lax.axis_size("tensor")
        self.place = lax.axis_index("tensor")
        self.behind = [
            jnp.where(self.place >= slot, self.place - slot, self.place - slot + self.count)
            for slot in range(self.count)
        ]

    def ahead(self, slot):
        return self.behind[(self.count - slot) % self.count]

    def gather_step(self, pair, step):
        count = self.count
        return (
            lax.ppermute(pair[0], "tensor", [(i, i + 1) for i in range(step - 1, count - 1)]),
            lax.ppermute(pair[1], "tensor", [(i, i - 1) for i in range(1, count - step + 1)]),
        )

    def reduce_step(self, pair, step):
        count = self.count
        return (
            lax.ppermute(pair[0], "tensor", [(i, i + 1) for i in range(step)]),
            lax.ppermute(pair[1], "tensor", [(i, i - 1) for i in range(count - step, count)]),
        )

    def slots(self, pairs):
        return [pairs[0][0]] + [
            jnp.where(self.place >= slot, pairs[slot][0], pairs[self.count - slot][1])
            for slot in range(1, self.count)
        ]


class Gather:
    def __init__(self, line, block, name):
        self.line = line
        self.name = name
        self.pairs = [(block, block)]

    def go(self, *after):
        step = len(self.pairs)
        if step < self.line.count:
            pair = tied(self.pairs[-1], *after)
            with jax.named_scope(f"{self.name}_gather_{step}"):
                moved = self.line.gather_step(pair, step)
            self.pairs.append(lax.optimization_barrier(moved))

    @property
    def last(self):
        return self.pairs[-1]

    def slots(self):
        while len(self.pairs) < self.line.count:
            self.go()
        return self.line.slots(self.pairs)


class Reduce:
    def __init__(self, line, part, name):
        self.line = line
        self.name = name
        self.part = part
        self.step = 0
        self.last = None
        self.sent = None

    def go(self, *after):
        count = self.line.count
        if self.step == count - 1:
            return
        pair = (self.part(count - 1 - self.step), self.part((self.step + 1) % count))
        if after:
            pair = tied(pair, *after)
        if self.last is not None:
            pair = (self.last[0] + pair[0], self.last[1] + pair[1])
        self.step += 1
        self.sent = pair = lax.optimization_barrier(pair)
        with jax.named_scope(f"{self.name}_sum_{self.step}"):
            moved = self.line.reduce_step(pair, self.step)
        self.last = lax.optimization_barrier(moved)

    def total(self, *after):
        while self.step < self.line.count - 1:
            self.go()
        pair = tied(self.last, *after)
        return self.part(0) + pair[0] + pair[1]


def row_block(values, start, rows):
    return lax.dynamic_slice_in_dim(values, start, rows, axis=0)


def tied(values, *before):
    return lax.optimization_barrier((values, before))[0]


def shards(
    tokens,
    positions,
    span_starts,
    attention_gain,
    query_weight,
    key_matrix,
    value_matrix,
    query_gain,
    key_gain,
    output_weight,
    feedforward_gain,
    gate_weight,
    up_weight,
    down_weight,
    cotangent,
):
    low = jnp.bfloat16
    line = Line()
    ranks = line.count
    place = line.place
    groups = lax.axis_size("dp")
    group = lax.axis_index("dp")
    seq_length = positions.shape[1]
    head_size = query_gain.shape[0]
    model_width, local_width = query_weight.shape
    query_heads = local_width // head_size
    kv_heads = key_matrix.shape[1] // head_size
    group_size = query_heads // kv_heads
    score_scale = head_size ** (-0.5)
    attention_gain_f = attention_gain.astype(jnp.float32)
    feedforward_gain_f = feedforward_gain.astype(jnp.float32)
    query_gain_f = query_gain.astype(jnp.float32)
    key_gain_f = key_gain.astype(jnp.float32)

    unit = jnp.where(positions[0, 0] >= 0, 1.0, 0.0)

    weight_rows = local_width // groups
    own_rows = row_block(output_weight, group * weight_rows, weight_rows).astype(jnp.float32)
    weight_by_rank = lax.all_gather(own_rows, "tensor", axis=0)

    inputs = tokens.astype(jnp.float32)
    normalized_rows, factor_one = norm_rows(inputs, attention_gain_f)
    normed_low = normalized_rows.astype(low)
    query_raw = jnp.dot(normed_low, query_weight, preferred_element_type=jnp.float32).reshape(
        seq_length, query_heads, head_size
    )
    key_unrotated = jnp.dot(normed_low, key_matrix, preferred_element_type=jnp.float32).reshape(
        seq_length, kv_heads, head_size
    )
    value_low = jnp.dot(normed_low, value_matrix, preferred_element_type=jnp.float32).astype(low)
    frequency = jnp.exp(
        jnp.arange(head_size // 2, dtype=jnp.float32) * (-2.0 * math.log(rope_base) / head_size)
    )
    angles = positions.astype(jnp.float32).reshape(seq_length)[:, None] * frequency
    cosine = jnp.cos(angles)[:, None, :]
    sine = jnp.sin(angles)[:, None, :]
    query_normed, query_factor = norm_rows(query_raw, query_gain_f)
    key_normed, key_factor = norm_rows(key_unrotated, key_gain_f)
    query_low = rotate_half(query_normed, cosine, sine).astype(low)
    key_low = rotate_half(key_normed, cosine, sine).astype(low)
    query_all = query_low.reshape(seq_length, kv_heads, group_size, head_size)
    key_all = key_low.reshape(seq_length, kv_heads, head_size)
    value_all = value_low.reshape(seq_length, kv_heads, head_size)
    mask = span_mask(span_starts[0], seq_length)

    late = slice(HALF, seq_length)
    early = slice(0, HALF)
    seen = {0: slice(0, seq_length), 1: early}
    rows_of = {0: late, 1: early}
    share_of = {0: (seq_length - HALF) // ranks, 1: HALF // ranks}

    def part_of(values, share):
        return lambda slot: row_block(values, line.ahead(slot) * share, share)

    def in_order(slots, buffer=None, first=0):
        share, width = slots[0].shape
        if buffer is None:
            buffer = jnp.zeros((share * ranks, width), low)
        for slot in range(ranks):
            buffer = lax.dynamic_update_slice_in_dim(
                buffer, (slots[slot] * unit).astype(low), first + line.behind[slot] * share, axis=0
            )
        return buffer

    def forward_half(half, query_rows):
        mixed, log_total = attend(
            query_rows,
            key_all[seen[half]],
            value_all[seen[half]],
            mask[rows_of[half], seen[half]],
            score_scale,
        )
        return mixed.reshape(-1, local_width), log_total

    mixed_0, total_0 = forward_half(0, query_all[late])
    heads_0 = Gather(line, mixed_0, "heads_0")
    heads_0.go()
    mixed_1, total_1 = forward_half(1, tied(query_all[early], mixed_0))
    log_total = {0: total_0, 1: total_1}
    heads_1 = Gather(line, mixed_1, "heads_1")
    other_rows = jnp.concatenate(
        [row_block(tied(weight_by_rank, mixed_1), line.behind[slot], 1) for slot in range(1, ranks)]
    )
    gathered_weight = lax.all_gather(other_rows, "dp", axis=0)
    first_step = heads_0.last
    heads_0.go()
    grad_hidden = contract(tied(cotangent, mixed_1, first_step), down_weight, 1, 1)
    second_step = heads_0.last
    heads_0.go(grad_hidden)
    gathered_weight = tied(gathered_weight, grad_hidden)
    whole_weight = jnp.concatenate(
        [output_weight]
        + [
            (gathered_weight[:, slot - 1].reshape(local_width, model_width) * unit).astype(low)
            for slot in range(1, ranks)
        ],
        axis=0,
    )
    heads_1.go(second_step, whole_weight)

    def whole_heads(slots):
        return jnp.concatenate([(block * unit).astype(low) for block in slots], axis=1)

    def residual_rows(half, mixed_whole):
        residual = tokens[rows_of[half]].astype(jnp.float32) + jnp.dot(
            mixed_whole, whole_weight, preferred_element_type=jnp.float32
        )
        normed_two, factor_two = norm_rows(residual, feedforward_gain_f)
        return residual, factor_two, normed_two.astype(low)

    def gate_up(normed_two_low):
        return (
            jnp.dot(normed_two_low, gate_weight, preferred_element_type=jnp.float32),
            jnp.dot(normed_two_low, up_weight, preferred_element_type=jnp.float32),
        )

    def feed_forward(half, gate_values, up_values, between=None):
        sigmoid_gate = jax.nn.sigmoid(gate_values)
        silu_gate = gate_values * sigmoid_gate
        hidden_low = (silu_gate * up_values).astype(low)
        grad_hidden_rows = grad_hidden[rows_of[half]]
        grad_gate = (
            grad_hidden_rows * up_values * sigmoid_gate * (1.0 + gate_values * (1.0 - sigmoid_gate))
        ).astype(low)
        grad_up = (grad_hidden_rows * silu_gate).astype(low)
        if between is not None:
            grad_gate, grad_up = tied((grad_gate, grad_up), between(hidden_low))
        grad_normed_part = contract(grad_gate, gate_weight, 1, 1) + contract(
            grad_up, up_weight, 1, 1
        )
        return hidden_low, grad_gate, grad_up, grad_normed_part

    def own_rows_back(half, residual, factor_two, grad_normed_two):
        share = share_of[half]
        own_first = place * share
        own_residual = row_block(residual, own_first, share)
        grad_norm, gain_rows = norm_back(
            own_residual,
            row_block(factor_two, own_first, share),
            feedforward_gain_f,
            grad_normed_two,
        )
        grad_residual = (
            row_block(cotangent[rows_of[half]], own_first, share).astype(jnp.float32) + grad_norm
        )
        grad_residual_low = grad_residual.astype(low)
        grad_mixed_own = contract(grad_residual_low, whole_weight, 1, 1)
        return grad_residual, grad_residual_low, jnp.sum(gain_rows, axis=0), grad_mixed_own

    def swap_heads(grad_mixed_own, *before):
        blocks = []
        for slot in range(ranks):
            first = (ranks - slot) % ranks * local_width
            piece = grad_mixed_own[:, first : first + local_width]
            if slot:
                piece = lax.ppermute(
                    piece, "tensor", [(i, (i + slot) % ranks) for i in range(ranks)]
                )
            blocks.append(piece)
        return in_order(tied(blocks, *before))

    mixed_whole_0 = whole_heads(tied(heads_0.slots(), whole_weight))
    residual_0, factor_0, normed_0 = residual_rows(0, mixed_whole_0)
    gate_0, up_0 = gate_up(normed_0)
    gate_0, up_0 = tied((gate_0, up_0), heads_1.last)
    heads_1.go(gate_0)
    hidden_0, grad_gate_0, grad_up_0, part_0 = feed_forward(0, gate_0, up_0)
    normed_sum_0 = Reduce(line, part_of(part_0, share_of[0]), "normed_0")
    normed_sum_0.go()
    first_step = heads_1.last
    heads_1.go(part_0)
    down_part_0 = jnp.dot(tied(hidden_0, part_0, first_step), down_weight, preferred_element_type=jnp.float32)

    mixed_whole_1 = whole_heads(tied(heads_1.slots(), down_part_0))
    normed_sum_0.go(down_part_0)
    residual_1, factor_1, normed_1 = residual_rows(1, tied(mixed_whole_1, normed_sum_0.sent))
    normed_sum_0.go(residual_1)
    gate_1, up_1 = gate_up(normed_1)
    down_sum_0 = Reduce(line, part_of(down_part_0, share_of[0]), "down_0")
    stages = []

    def late_sums(hidden_1):
        hidden = jnp.concatenate([hidden_1, hidden_0], axis=0)
        down_grad = contract(hidden, cotangent, 0, 0)
        down_sum_0.go(normed_sum_0.last, gate_1)
        back = own_rows_back(0, residual_0, factor_0, normed_sum_0.total(down_sum_0.sent))
        stages.extend([down_grad, back])
        return down_grad, back[3], down_sum_0.last

    hidden_1, grad_gate_1, grad_up_1, part_1 = feed_forward(1, gate_1, up_1, late_sums)
    down_grad, back_0 = stages
    down_share = lax.psum_scatter(
        tied(down_grad, down_sum_0.last), "dp", scatter_dimension=1, tiled=True
    )
    down_sum_0.go(back_0[3])
    normed_sum_1 = Reduce(line, part_of(part_1, share_of[1]), "normed_1")
    down_part_1 = jnp.dot(tied(hidden_1, part_1), down_weight, preferred_element_type=jnp.float32)
    grad_mixed_0 = swap_heads(back_0[3], down_part_1)
    down_sum_0.go(grad_mixed_0)
    normed_two = jnp.concatenate([normed_1, normed_0], axis=0)
    grad_gate_up = jnp.concatenate(
        [
            jnp.concatenate([grad_gate_1, grad_up_1], axis=1),
            jnp.concatenate([grad_gate_0, grad_up_0], axis=1),
        ],
        axis=0,
    )
    gate_up_grad = contract(tied(normed_two, down_sum_0.sent), grad_gate_up, 0, 0)
    hidden_width = gate_weight.shape[1]
    down_sum_1 = Reduce(line, part_of(down_part_1, share_of[1]), "down_1")

    def attention_core(half, grad_mixed):
        rows = rows_of[half]
        count = rows.stop - rows.start
        return attend_back(
            query_all[rows],
            key_all[seen[half]],
            value_all[seen[half]],
            mask[rows, seen[half]],
            log_total[half],
            grad_mixed.reshape(count, kv_heads, group_size, head_size),
            score_scale,
        )

    def attention_rest(half, core, extra, *before):
        rows = rows_of[half]
        count = rows.stop - rows.start
        grad_query_rot, grad_key_rot, grad_value = core
        if extra is None:
            rest = (grad_key_rot[early], grad_value[early])
            grad_key_rot = grad_key_rot[late]
            grad_value = grad_value[late]
        else:
            rest = None
            grad_key_rot = grad_key_rot + extra[0]
            grad_value = grad_value + extra[1]
        grad_query_norm = rotate_back(
            grad_query_rot.reshape(count, query_heads, head_size), cosine[rows], sine[rows]
        )
        grad_key_norm = rotate_back(
            grad_key_rot.reshape(count, kv_heads, head_size), cosine[rows], sine[rows]
        )
        grad_query_raw, query_gain_rows = norm_back(
            query_raw[rows], query_factor[rows], query_gain_f, grad_query_norm
        )
        grad_key_raw, key_gain_rows = norm_back(
            key_unrotated[rows], key_factor[rows], key_gain_f, grad_key_norm
        )
        gains = (jnp.sum(query_gain_rows, axis=(0, 1)), jnp.sum(key_gain_rows, axis=(0, 1)))
        grad_query_low = grad_query_raw.reshape(count, local_width).astype(low)
        grad_key_low = grad_key_raw.reshape(count, kv_heads * head_size).astype(low)
        grad_value_low = grad_value.reshape(count, kv_heads * head_size).astype(low)
        if before:
            grad_query_low = tied(grad_query_low, *before)
        grad_input_part = (
            contract(grad_query_low, query_weight, 1, 1)
            + contract(grad_key_low, key_matrix, 1, 1)
            + contract(grad_value_low, value_matrix, 1, 1)
        )
        grads = jnp.concatenate([grad_query_low, grad_key_low, grad_value_low], axis=1)
        return rest, gains, grads, grad_input_part

    def tokens_back(half, grad_residual, grad_normed_one):
        share = share_of[half]
        own_first = rows_of[half].start + place * share
        grad_norm, gain_rows = norm_back(
            row_block(tokens, own_first, share).astype(jnp.float32),
            row_block(factor_one, own_first, share),
            attention_gain_f,
            grad_normed_one,
        )
        return grad_residual + grad_norm, jnp.sum(gain_rows, axis=0)

    def own_block(half, residual, down_sum):
        return Gather(
            line,
            row_block(residual, place * share_of[half], share_of[half]) + down_sum.total(),
            f"block_{half}",
        )

    block_0 = own_block(0, residual_0, down_sum_0)
    block_0.go(gate_up_grad)
    gate_up_share = lax.psum_scatter(
        tied(gate_up_grad, down_share, block_0.last), "dp", scatter_dimension=0, tiled=True
    )
    before = (block_0.last,)
    normed_sum_1.go(*before)
    block_0.go(*before)
    core_0 = attention_core(0, tied(grad_mixed_0, gate_up_grad, normed_sum_1.sent))
    before = (normed_sum_1.last, block_0.last)
    normed_sum_1.go(*before)
    block_0.go(*before)
    rest, gains_0, grads_0, input_part_0 = attention_rest(
        0, tied(core_0, normed_sum_1.sent), None
    )
    input_sum_0 = Reduce(line, part_of(input_part_0, share_of[0]), "input_0")
    before = (normed_sum_1.last, block_0.last)
    normed_sum_1.go(*before)
    back_1 = own_rows_back(1, residual_1, factor_1, normed_sum_1.total())
    grad_mixed_1 = swap_heads(back_1[3])
    input_sum_0.go(back_1[3])

    def natural(mixed_whole, half):
        own = row_block(mixed_whole, place * share_of[half], share_of[half])
        return jnp.concatenate(
            [
                lax.dynamic_slice_in_dim(
                    own,
                    jnp.where(place >= rank, place - rank, place - rank + ranks) * local_width,
                    local_width,
                    axis=1,
                )
                for rank in range(ranks)
            ],
            axis=1,
        )

    output_grad = contract(
        jnp.concatenate([natural(mixed_whole_0, 0), natural(mixed_whole_1, 1)], axis=0),
        tied(jnp.concatenate([back_0[1], back_1[1]], axis=0), back_1[3]),
        0,
        0,
    )

    input_sum_0.go(grad_mixed_1)
    core_1 = attention_core(1, tied(grad_mixed_1, input_sum_0.sent))
    _, gains_1, grads_1, input_part_1 = attention_rest(1, core_1, rest)
    input_sum_1 = Reduce(line, part_of(input_part_1, share_of[1]), "input_1")
    tokens_own_0, attention_gain_0 = tokens_back(0, back_0[0], input_sum_0.total())
    output_part = lax.psum_scatter(
        tied(output_grad, gate_up_share, tokens_own_0),
        "dp",
        scatter_dimension=1,
        tiled=True,
    )
    tokens_0 = Gather(line, tokens_own_0, "tokens_0")
    tokens_0.go()
    qkv_grad = contract(
        tied(normed_low, tokens_own_0),
        jnp.concatenate([grads_1, grads_0], axis=0),
        0,
        0,
    )
    key_width = kv_heads * head_size

    before = (tokens_0.last,)
    down_sum_1.go(*before)
    tokens_0.go(*before)
    before = (tokens_0.last, down_sum_1.last)
    down_sum_1.go(*before)
    tokens_0.go(*before)
    before = (tokens_0.last, down_sum_1.last)
    down_sum_1.go(*before)
    block_1 = own_block(1, residual_1, down_sum_1)
    block_1.go()
    qkv_share = lax.psum_scatter(
        tied(qkv_grad, output_part, block_1.last), "dp", scatter_dimension=0, tiled=True
    )
    before = (block_1.last,)
    input_sum_1.go(*before)
    block_1.go(*before)
    before = (input_sum_1.last, block_1.last)
    input_sum_1.go(*before)
    block_1.go(*before)
    before = (input_sum_1.last, block_1.last)
    input_sum_1.go(*before)
    tokens_own_1, attention_gain_1 = tokens_back(1, back_1[0], input_sum_1.total())
    tokens_1 = Gather(line, tokens_own_1, "tokens_1")
    gains = jnp.concatenate(
        [
            attention_gain_0 + attention_gain_1,
            back_0[2] + back_1[2],
            gains_0[0] + gains_1[0],
            gains_0[1] + gains_1[1],
        ]
    )

    exchanges = [("dp", groups, 1 << bit) for bit in range((groups - 1).bit_length())]
    exchanges += [("tensor", ranks, 1 << bit) for bit in range((ranks - 1).bit_length())]
    output_sum = Reduce(line, part_of(output_part, local_width), "output")
    while len(tokens_1.pairs) < ranks or exchanges:
        tokens_1.go()
        if len(tokens_1.pairs) > 2:
            output_sum.go(tokens_1.pairs[-2])
            tokens_1.pairs[-1], output_sum.last = lax.optimization_barrier(
                (tokens_1.last, output_sum.last)
            )
        for axis, size, distance in exchanges[:2]:
            gains = gains + lax.ppermute(gains, axis, [(i, i ^ distance) for i in range(size)])
        exchanges = exchanges[2:]
        tokens_1.pairs[-1], gains = lax.optimization_barrier((tokens_1.last, gains))

    tokens_grad = jnp.zeros((seq_length, model_width), low)
    tokens_grad = in_order(tokens_0.slots(), tokens_grad, HALF)
    block_output = jnp.zeros((seq_length, model_width), low)
    block_output = in_order(block_0.slots(), block_output, HALF)
    block_output = in_order(block_1.slots(), block_output, 0)
    shares = (
        qkv_share[:, :local_width],
        qkv_share[:, local_width : local_width + key_width],
        qkv_share[:, local_width + key_width :],
        gate_up_share[:, :hidden_width],
        gate_up_share[:, hidden_width:],
    )
    output_sum.go()
    output_share = output_sum.total(shares, block_output)
    last_slots = tokens_1.slots()
    tokens_grad = in_order(last_slots, tokens_grad, 0)

    def gain_share(first, size):
        part = size // groups
        return lax.dynamic_slice_in_dim(gains, first + group * part, part, axis=0)

    return (
        block_output,
        tokens_grad,
        gain_share(0, model_width),
        shares[0],
        shares[1],
        shares[2],
        gain_share(2 * model_width, head_size),
        gain_share(2 * model_width + head_size, head_size),
        output_share,
        gain_share(model_width, model_width),
        shares[3],
        shares[4],
        down_share,
    )


def solution(mesh):
    return jax.shard_map(
        shards,
        mesh=mesh,
        in_specs=(
            P("dp", None),
            P("dp", None),
            P("dp", None),
            P(),
            P(None, "tensor"),
            P(None, "tensor"),
            P(None, "tensor"),
            P(),
            P(),
            P("tensor", None),
            P(),
            P(None, "tensor"),
            P(None, "tensor"),
            P("tensor", None),
            P("dp", None),
        ),
        out_specs=(
            P("dp", None),
            P("dp", None),
            P("dp"),
            P("dp", "tensor"),
            P("dp", "tensor"),
            P("dp", "tensor"),
            P("dp"),
            P("dp"),
            P("tensor", "dp"),
            P("dp"),
            P("dp", "tensor"),
            P("dp", "tensor"),
            P("tensor", "dp"),
        ),
        check_vma=False,
    )
```

```python
import math

import jax
import jax.numpy as jnp
from jax import lax
from jax.sharding import PartitionSpec as P

SPAN = 256
HALF = 512

epsilon = 1e-06
rope_base = 1000000.0


def contract(left, right, left_dim, right_dim):
    return lax.dot_general(
        left, right, (((left_dim,), (right_dim,)), ((), ())), preferred_element_type=jnp.float32
    )


def norm_rows(values, gain):
    factor = lax.rsqrt(jnp.mean(values * values, axis=-1, keepdims=True) + epsilon)
    return (values * factor * gain, factor)


def norm_back(values, factor, gain, grad_out):
    scaled = grad_out * gain
    inner_sum = jnp.sum(scaled * values, axis=-1, keepdims=True)
    grad_in = factor * scaled - values * (factor * factor * factor) * inner_sum / values.shape[-1]
    return (grad_in, grad_out * values * factor)


def rotate_half(values, cosine, sine):
    half_size = values.shape[-1] // 2
    first_half = values[..., :half_size]
    second_half = values[..., half_size:]
    return jnp.concatenate(
        [first_half * cosine - second_half * sine, second_half * cosine + first_half * sine],
        axis=-1,
    )


def rotate_back(values, cosine, sine):
    half_size = values.shape[-1] // 2
    first_half = values[..., :half_size]
    second_half = values[..., half_size:]
    return jnp.concatenate(
        [first_half * cosine + second_half * sine, second_half * cosine - first_half * sine],
        axis=-1,
    )


def span_mask(starts, seq_length):
    token_index = jnp.arange(seq_length, dtype=jnp.int32)
    inside = (token_index[None, :] >= starts[:, None]) & (
        token_index[None, :] < starts[:, None] + SPAN
    )
    span_number = jnp.arange(starts.shape[0], dtype=jnp.int32)[:, None] + 1
    span_label = jnp.sum(inside.astype(jnp.int32) * span_number, axis=0)
    causal = token_index[:, None] >= token_index[None, :]
    same_span = (span_label[:, None] == span_label[None, :]) & (span_label[:, None] > 0)
    return causal | same_span


def score_block(query_rows, key_heads, allowed, score_scale):
    scores = (
        jnp.einsum("qhgd,khd->hgqk", query_rows, key_heads, preferred_element_type=jnp.float32)
        * score_scale
    )
    return jnp.where(allowed, scores, -jnp.inf)


def attend(query_rows, key_heads, heads_value, allowed, score_scale):
    scores = score_block(query_rows, key_heads, allowed, score_scale)
    highest = jnp.max(scores, axis=-1, keepdims=True)
    exponent = jnp.exp(scores - highest)
    denominator = jnp.sum(exponent, axis=-1, keepdims=True)
    probability = (exponent / denominator).astype(jnp.bfloat16)
    mixed_heads = jnp.einsum(
        "hgqk,khd->qhgd", probability, heads_value, preferred_element_type=jnp.float32
    )
    return (mixed_heads, (highest + jnp.log(denominator))[..., 0])


def attend_back(query_rows, key_heads, heads_value, allowed, log_total, grad_mixed, score_scale):
    scores = score_block(query_rows, key_heads, allowed, score_scale)
    probability = jnp.exp(scores - log_total[..., None])
    grad_value = jnp.einsum(
        "hgqk,qhgd->khd",
        probability.astype(jnp.bfloat16),
        grad_mixed,
        preferred_element_type=jnp.float32,
    )
    grad_prob = jnp.einsum(
        "qhgd,khd->hgqk", grad_mixed, heads_value, preferred_element_type=jnp.float32
    )
    grad_scores = probability * (
        grad_prob - jnp.sum(probability * grad_prob, axis=-1, keepdims=True)
    )
    grad_low = grad_scores.astype(jnp.bfloat16)
    grad_queries = (
        jnp.einsum("hgqk,khd->qhgd", grad_low, key_heads, preferred_element_type=jnp.float32)
        * score_scale
    )
    grad_keys = (
        jnp.einsum("hgqk,qhgd->khd", grad_low, query_rows, preferred_element_type=jnp.float32)
        * score_scale
    )
    return (grad_queries, grad_keys, grad_value)


class Line:
    def __init__(self):
        self.count = lax.axis_size("tensor")
        self.place = lax.axis_index("tensor")
        self.behind = [
            jnp.where(self.place >= slot, self.place - slot, self.place - slot + self.count)
            for slot in range(self.count)
        ]

    def ahead(self, slot):
        return self.behind[(self.count - slot) % self.count]

    def gather_step(self, pair, step):
        count = self.count
        return (
            lax.ppermute(pair[0], "tensor", [(i, i + 1) for i in range(step - 1, count - 1)]),
            lax.ppermute(pair[1], "tensor", [(i, i - 1) for i in range(1, count - step + 1)]),
        )

    def reduce_step(self, pair, step):
        count = self.count
        return (
            lax.ppermute(pair[0], "tensor", [(i, i + 1) for i in range(step)]),
            lax.ppermute(pair[1], "tensor", [(i, i - 1) for i in range(count - step, count)]),
        )

    def slots(self, pairs):
        return [pairs[0][0]] + [
            jnp.where(self.place >= slot, pairs[slot][0], pairs[self.count - slot][1])
            for slot in range(1, self.count)
        ]


class Gather:
    def __init__(self, line, block, name):
        self.line = line
        self.name = name
        self.pairs = [(block, block)]

    def go(self, *after):
        step = len(self.pairs)
        if step < self.line.count:
            pair = tied(self.pairs[-1], *after)
            with jax.named_scope(f"{self.name}_gather_{step}"):
                moved = self.line.gather_step(pair, step)
            self.pairs.append(lax.optimization_barrier(moved))

    @property
    def last(self):
        return self.pairs[-1]

    def slots(self):
        while len(self.pairs) < self.line.count:
            self.go()
        return self.line.slots(self.pairs)


class Reduce:
    def __init__(self, line, part, name):
        self.line = line
        self.name = name
        self.part = part
        self.step = 0
        self.last = None
        self.sent = None

    def go(self, *after):
        count = self.line.count
        if self.step == count - 1:
            return
        pair = (self.part(count - 1 - self.step), self.part((self.step + 1) % count))
        if after:
            pair = tied(pair, *after)
        if self.last is not None:
            pair = (self.last[0] + pair[0], self.last[1] + pair[1])
        self.step += 1
        self.sent = pair = lax.optimization_barrier(pair)
        with jax.named_scope(f"{self.name}_sum_{self.step}"):
            moved = self.line.reduce_step(pair, self.step)
        self.last = lax.optimization_barrier(moved)

    def total(self, *after):
        while self.step < self.line.count - 1:
            self.go()
        pair = tied(self.last, *after)
        return self.part(0) + pair[0] + pair[1]


def row_block(values, start, rows):
    return lax.dynamic_slice_in_dim(values, start, rows, axis=0)


def tied(values, *before):
    return lax.optimization_barrier((values, before))[0]


def shards(
    tokens,
    positions,
    span_starts,
    attention_gain,
    query_weight,
    key_matrix,
    value_matrix,
    query_gain,
    key_gain,
    output_weight,
    feedforward_gain,
    gate_weight,
    up_weight,
    down_weight,
    cotangent,
):
    low = jnp.bfloat16
    line = Line()
    ranks = line.count
    place = line.place
    groups = lax.axis_size("dp")
    group = lax.axis_index("dp")
    seq_length = positions.shape[1]
    head_size = query_gain.shape[0]
    model_width, local_width = query_weight.shape
    query_heads = local_width // head_size
    kv_heads = key_matrix.shape[1] // head_size
    group_size = query_heads // kv_heads
    score_scale = head_size ** (-0.5)
    attention_gain_f = attention_gain.astype(jnp.float32)
    feedforward_gain_f = feedforward_gain.astype(jnp.float32)
    query_gain_f = query_gain.astype(jnp.float32)
    key_gain_f = key_gain.astype(jnp.float32)

    unit = jnp.where(positions[0, 0] >= 0, 1.0, 0.0)

    weight_rows = local_width // groups
    own_rows = row_block(output_weight, group * weight_rows, weight_rows).astype(jnp.float32)
    weight_by_rank = lax.all_gather(own_rows, "tensor", axis=0)

    inputs = tokens.astype(jnp.float32)
    normalized_rows, factor_one = norm_rows(inputs, attention_gain_f)
    normed_low = normalized_rows.astype(low)
    query_raw = jnp.dot(normed_low, query_weight, preferred_element_type=jnp.float32).reshape(
        seq_length, query_heads, head_size
    )
    key_unrotated = jnp.dot(normed_low, key_matrix, preferred_element_type=jnp.float32).reshape(
        seq_length, kv_heads, head_size
    )
    value_low = jnp.dot(normed_low, value_matrix, preferred_element_type=jnp.float32).astype(low)
    frequency = jnp.exp(
        jnp.arange(head_size // 2, dtype=jnp.float32) * (-2.0 * math.log(rope_base) / head_size)
    )
    angles = positions.astype(jnp.float32).reshape(seq_length)[:, None] * frequency
    cosine = jnp.cos(angles)[:, None, :]
    sine = jnp.sin(angles)[:, None, :]
    query_normed, query_factor = norm_rows(query_raw, query_gain_f)
    key_normed, key_factor = norm_rows(key_unrotated, key_gain_f)
    query_low = rotate_half(query_normed, cosine, sine).astype(low)
    key_low = rotate_half(key_normed, cosine, sine).astype(low)
    query_all = query_low.reshape(seq_length, kv_heads, group_size, head_size)
    key_all = key_low.reshape(seq_length, kv_heads, head_size)
    value_all = value_low.reshape(seq_length, kv_heads, head_size)
    mask = span_mask(span_starts[0], seq_length)

    late = slice(HALF, seq_length)
    early = slice(0, HALF)
    seen = {0: slice(0, seq_length), 1: early}
    rows_of = {0: late, 1: early}
    share_of = {0: (seq_length - HALF) // ranks, 1: HALF // ranks}

    def part_of(values, share):
        return lambda slot: row_block(values, line.ahead(slot) * share, share)

    def in_order(slots, buffer=None, first=0):
        share, width = slots[0].shape
        if buffer is None:
            buffer = jnp.zeros((share * ranks, width), low)
        for slot in range(ranks):
            buffer = lax.dynamic_update_slice_in_dim(
                buffer, (slots[slot] * unit).astype(low), first + line.behind[slot] * share, axis=0
            )
        return buffer

    def forward_half(half, query_rows):
        mixed, log_total = attend(
            query_rows,
            key_all[seen[half]],
            value_all[seen[half]],
            mask[rows_of[half], seen[half]],
            score_scale,
        )
        return mixed.reshape(-1, local_width), log_total

    mixed_0, total_0 = forward_half(0, query_all[late])
    heads_0 = Gather(line, mixed_0, "heads_0")
    heads_0.go()
    mixed_1, total_1 = forward_half(1, tied(query_all[early], mixed_0))
    log_total = {0: total_0, 1: total_1}
    heads_1 = Gather(line, mixed_1, "heads_1")
    other_rows = jnp.concatenate(
        [row_block(tied(weight_by_rank, mixed_1), line.behind[slot], 1) for slot in range(1, ranks)]
    )
    gathered_weight = lax.all_gather(other_rows, "dp", axis=0)
    first_step = heads_0.last
    heads_0.go()
    grad_hidden = contract(tied(cotangent, mixed_1, first_step), down_weight, 1, 1)
    second_step = heads_0.last
    heads_0.go(grad_hidden)
    gathered_weight = tied(gathered_weight, grad_hidden)
    whole_weight = jnp.concatenate(
        [output_weight]
        + [
            (gathered_weight[:, slot - 1].reshape(local_width, model_width) * unit).astype(low)
            for slot in range(1, ranks)
        ],
        axis=0,
    )
    heads_1.go(second_step, whole_weight)

    def whole_heads(slots):
        return jnp.concatenate([(block * unit).astype(low) for block in slots], axis=1)

    def residual_rows(half, mixed_whole):
        residual = tokens[rows_of[half]].astype(jnp.float32) + jnp.dot(
            mixed_whole, whole_weight, preferred_element_type=jnp.float32
        )
        normed_two, factor_two = norm_rows(residual, feedforward_gain_f)
        return residual, factor_two, normed_two.astype(low)

    def gate_up(normed_two_low):
        return (
            jnp.dot(normed_two_low, gate_weight, preferred_element_type=jnp.float32),
            jnp.dot(normed_two_low, up_weight, preferred_element_type=jnp.float32),
        )

    def feed_forward(half, gate_values, up_values, between=None):
        sigmoid_gate = jax.nn.sigmoid(gate_values)
        silu_gate = gate_values * sigmoid_gate
        hidden_low = (silu_gate * up_values).astype(low)
        grad_hidden_rows = grad_hidden[rows_of[half]]
        grad_gate = (
            grad_hidden_rows * up_values * sigmoid_gate * (1.0 + gate_values * (1.0 - sigmoid_gate))
        ).astype(low)
        grad_up = (grad_hidden_rows * silu_gate).astype(low)
        if between is not None:
            grad_gate, grad_up = tied((grad_gate, grad_up), between(hidden_low))
        grad_normed_part = contract(grad_gate, gate_weight, 1, 1) + contract(
            grad_up, up_weight, 1, 1
        )
        return hidden_low, grad_gate, grad_up, grad_normed_part

    def own_rows_back(half, residual, factor_two, grad_normed_two):
        share = share_of[half]
        own_first = place * share
        own_residual = row_block(residual, own_first, share)
        grad_norm, gain_rows = norm_back(
            own_residual,
            row_block(factor_two, own_first, share),
            feedforward_gain_f,
            grad_normed_two,
        )
        grad_residual = (
            row_block(cotangent[rows_of[half]], own_first, share).astype(jnp.float32) + grad_norm
        )
        grad_residual_low = grad_residual.astype(low)
        grad_mixed_own = contract(grad_residual_low, whole_weight, 1, 1)
        return grad_residual, grad_residual_low, jnp.sum(gain_rows, axis=0), grad_mixed_own

    def swap_heads(grad_mixed_own, *before):
        blocks = []
        for slot in range(ranks):
            first = (ranks - slot) % ranks * local_width
            piece = grad_mixed_own[:, first : first + local_width]
            if slot:
                piece = lax.ppermute(
                    piece, "tensor", [(i, (i + slot) % ranks) for i in range(ranks)]
                )
            blocks.append(piece)
        return in_order(tied(blocks, *before))

    mixed_whole_0 = whole_heads(tied(heads_0.slots(), whole_weight))
    residual_0, factor_0, normed_0 = residual_rows(0, mixed_whole_0)
    gate_0, up_0 = gate_up(normed_0)
    gate_0, up_0 = tied((gate_0, up_0), heads_1.last)
    heads_1.go(gate_0)
    hidden_0, grad_gate_0, grad_up_0, part_0 = feed_forward(0, gate_0, up_0)
    normed_sum_0 = Reduce(line, part_of(part_0, share_of[0]), "normed_0")
    normed_sum_0.go()
    first_step = heads_1.last
    heads_1.go(part_0)
    down_part_0 = jnp.dot(tied(hidden_0, part_0, first_step), down_weight, preferred_element_type=jnp.float32)

    mixed_whole_1 = whole_heads(tied(heads_1.slots(), down_part_0))
    normed_sum_0.go()
    residual_1, factor_1, normed_1 = residual_rows(1, tied(mixed_whole_1, normed_sum_0.sent))
    normed_sum_0.go(residual_1)
    gate_1, up_1 = gate_up(normed_1)
    down_sum_0 = Reduce(line, part_of(down_part_0, share_of[0]), "down_0")
    stages = []

    def late_sums(hidden_1):
        hidden = jnp.concatenate([hidden_1, hidden_0], axis=0)
        down_grad = contract(hidden, cotangent, 0, 0)
        down_sum_0.go(normed_sum_0.last, gate_1)
        back = own_rows_back(0, residual_0, factor_0, normed_sum_0.total(down_sum_0.sent))
        stages.extend([down_grad, back])
        return down_grad, back[3], down_sum_0.last

    hidden_1, grad_gate_1, grad_up_1, part_1 = feed_forward(1, gate_1, up_1, late_sums)
    down_grad, back_0 = stages
    down_share = lax.psum_scatter(
        tied(down_grad, down_sum_0.last), "dp", scatter_dimension=1, tiled=True
    )
    down_sum_0.go(back_0[3])
    normed_sum_1 = Reduce(line, part_of(part_1, share_of[1]), "normed_1")
    down_part_1 = jnp.dot(tied(hidden_1, part_1), down_weight, preferred_element_type=jnp.float32)
    grad_mixed_0 = swap_heads(back_0[3], down_part_1)
    down_sum_0.go(grad_mixed_0)
    normed_two = jnp.concatenate([normed_1, normed_0], axis=0)
    grad_gate_up = jnp.concatenate(
        [
            jnp.concatenate([grad_gate_1, grad_up_1], axis=1),
            jnp.concatenate([grad_gate_0, grad_up_0], axis=1),
        ],
        axis=0,
    )
    gate_up_grad = contract(tied(normed_two, down_sum_0.sent), grad_gate_up, 0, 0)
    hidden_width = gate_weight.shape[1]
    down_sum_1 = Reduce(line, part_of(down_part_1, share_of[1]), "down_1")

    def attention_core(half, grad_mixed):
        rows = rows_of[half]
        count = rows.stop - rows.start
        return attend_back(
            query_all[rows],
            key_all[seen[half]],
            value_all[seen[half]],
            mask[rows, seen[half]],
            log_total[half],
            grad_mixed.reshape(count, kv_heads, group_size, head_size),
            score_scale,
        )

    def attention_rest(half, core, extra, *before):
        rows = rows_of[half]
        count = rows.stop - rows.start
        grad_query_rot, grad_key_rot, grad_value = core
        if extra is None:
            rest = (grad_key_rot[early], grad_value[early])
            grad_key_rot = grad_key_rot[late]
            grad_value = grad_value[late]
        else:
            rest = None
            grad_key_rot = grad_key_rot + extra[0]
            grad_value = grad_value + extra[1]
        grad_query_norm = rotate_back(
            grad_query_rot.reshape(count, query_heads, head_size), cosine[rows], sine[rows]
        )
        grad_key_norm = rotate_back(
            grad_key_rot.reshape(count, kv_heads, head_size), cosine[rows], sine[rows]
        )
        grad_query_raw, query_gain_rows = norm_back(
            query_raw[rows], query_factor[rows], query_gain_f, grad_query_norm
        )
        grad_key_raw, key_gain_rows = norm_back(
            key_unrotated[rows], key_factor[rows], key_gain_f, grad_key_norm
        )
        gains = (jnp.sum(query_gain_rows, axis=(0, 1)), jnp.sum(key_gain_rows, axis=(0, 1)))
        grad_query_low = grad_query_raw.reshape(count, local_width).astype(low)
        grad_key_low = grad_key_raw.reshape(count, kv_heads * head_size).astype(low)
        grad_value_low = grad_value.reshape(count, kv_heads * head_size).astype(low)
        if before:
            grad_query_low = tied(grad_query_low, *before)
        grad_input_part = (
            contract(grad_query_low, query_weight, 1, 1)
            + contract(grad_key_low, key_matrix, 1, 1)
            + contract(grad_value_low, value_matrix, 1, 1)
        )
        grads = jnp.concatenate([grad_query_low, grad_key_low, grad_value_low], axis=1)
        return rest, gains, grads, grad_input_part

    def tokens_back(half, grad_residual, grad_normed_one):
        share = share_of[half]
        own_first = rows_of[half].start + place * share
        grad_norm, gain_rows = norm_back(
            row_block(tokens, own_first, share).astype(jnp.float32),
            row_block(factor_one, own_first, share),
            attention_gain_f,
            grad_normed_one,
        )
        return grad_residual + grad_norm, jnp.sum(gain_rows, axis=0)

    def own_block(half, residual, down_sum):
        return Gather(
            line,
            row_block(residual, place * share_of[half], share_of[half]) + down_sum.total(),
            f"block_{half}",
        )

    block_0 = own_block(0, residual_0, down_sum_0)
    block_0.go(gate_up_grad)
    gate_up_share = lax.psum_scatter(
        tied(gate_up_grad, down_share, block_0.last), "dp", scatter_dimension=0, tiled=True
    )
    before = (block_0.last,)
    normed_sum_1.go(*before)
    block_0.go(*before)
    core_0 = attention_core(0, tied(grad_mixed_0, gate_up_grad, normed_sum_1.sent))
    before = (normed_sum_1.last, block_0.last)
    normed_sum_1.go(*before)
    block_0.go(*before)
    rest, gains_0, grads_0, input_part_0 = attention_rest(
        0, tied(core_0, normed_sum_1.sent), None
    )
    input_sum_0 = Reduce(line, part_of(input_part_0, share_of[0]), "input_0")
    before = (normed_sum_1.last, block_0.last)
    normed_sum_1.go(*before)
    back_1 = own_rows_back(1, residual_1, factor_1, normed_sum_1.total())
    grad_mixed_1 = swap_heads(back_1[3])
    input_sum_0.go(back_1[3])

    def natural(mixed_whole, half):
        own = row_block(mixed_whole, place * share_of[half], share_of[half])
        return jnp.concatenate(
            [
                lax.dynamic_slice_in_dim(
                    own,
                    jnp.where(place >= rank, place - rank, place - rank + ranks) * local_width,
                    local_width,
                    axis=1,
                )
                for rank in range(ranks)
            ],
            axis=1,
        )

    output_grad = contract(
        jnp.concatenate([natural(mixed_whole_0, 0), natural(mixed_whole_1, 1)], axis=0),
        tied(jnp.concatenate([back_0[1], back_1[1]], axis=0), back_1[3]),
        0,
        0,
    )

    input_sum_0.go(grad_mixed_1)
    core_1 = attention_core(1, tied(grad_mixed_1, input_sum_0.sent))
    _, gains_1, grads_1, input_part_1 = attention_rest(1, core_1, rest)
    input_sum_1 = Reduce(line, part_of(input_part_1, share_of[1]), "input_1")
    tokens_own_0, attention_gain_0 = tokens_back(0, back_0[0], input_sum_0.total())
    output_part = lax.psum_scatter(
        tied(output_grad, gate_up_share, tokens_own_0),
        "dp",
        scatter_dimension=1,
        tiled=True,
    )
    tokens_0 = Gather(line, tokens_own_0, "tokens_0")
    tokens_0.go()
    qkv_grad = contract(
        tied(normed_low, tokens_own_0),
        jnp.concatenate([grads_1, grads_0], axis=0),
        0,
        0,
    )
    key_width = kv_heads * head_size

    before = (tokens_0.last,)
    down_sum_1.go(*before)
    tokens_0.go(*before)
    before = (tokens_0.last, down_sum_1.last)
    down_sum_1.go(*before)
    tokens_0.go(*before)
    before = (tokens_0.last, down_sum_1.last)
    down_sum_1.go(*before)
    block_1 = own_block(1, residual_1, down_sum_1)
    block_1.go()
    qkv_share = lax.psum_scatter(
        tied(qkv_grad, output_part, block_1.last), "dp", scatter_dimension=0, tiled=True
    )
    before = (block_1.last,)
    input_sum_1.go(*before)
    block_1.go(*before)
    before = (input_sum_1.last, block_1.last)
    input_sum_1.go(*before)
    block_1.go(*before)
    before = (input_sum_1.last, block_1.last)
    input_sum_1.go(*before)
    tokens_own_1, attention_gain_1 = tokens_back(1, back_1[0], input_sum_1.total())
    tokens_1 = Gather(line, tokens_own_1, "tokens_1")
    gains = jnp.concatenate(
        [
            attention_gain_0 + attention_gain_1,
            back_0[2] + back_1[2],
            gains_0[0] + gains_1[0],
            gains_0[1] + gains_1[1],
        ]
    )

    exchanges = [("dp", groups, 1 << bit) for bit in range((groups - 1).bit_length())]
    exchanges += [("tensor", ranks, 1 << bit) for bit in range((ranks - 1).bit_length())]
    output_sum = Reduce(line, part_of(output_part, local_width), "output")
    while len(tokens_1.pairs) < ranks or exchanges:
        tokens_1.go()
        if len(tokens_1.pairs) > 2:
            output_sum.go(tokens_1.pairs[-2])
            tokens_1.pairs[-1], output_sum.last = lax.optimization_barrier(
                (tokens_1.last, output_sum.last)
            )
        for axis, size, distance in exchanges[:2]:
            gains = gains + lax.ppermute(gains, axis, [(i, i ^ distance) for i in range(size)])
        exchanges = exchanges[2:]
        tokens_1.pairs[-1], gains = lax.optimization_barrier((tokens_1.last, gains))

    tokens_grad = jnp.zeros((seq_length, model_width), low)
    tokens_grad = in_order(tokens_0.slots(), tokens_grad, HALF)
    block_output = jnp.zeros((seq_length, model_width), low)
    block_output = in_order(block_0.slots(), block_output, HALF)
    block_output = in_order(block_1.slots(), block_output, 0)
    shares = (
        qkv_share[:, :local_width],
        qkv_share[:, local_width : local_width + key_width],
        qkv_share[:, local_width + key_width :],
        gate_up_share[:, :hidden_width],
        gate_up_share[:, hidden_width:],
    )
    output_sum.go()
    output_share = output_sum.total(shares, block_output)
    last_slots = tokens_1.slots()
    tokens_grad = in_order(last_slots, tokens_grad, 0)

    def gain_share(first, size):
        part = size // groups
        return lax.dynamic_slice_in_dim(gains, first + group * part, part, axis=0)

    return (
        block_output,
        tokens_grad,
        gain_share(0, model_width),
        shares[0],
        shares[1],
        shares[2],
        gain_share(2 * model_width, head_size),
        gain_share(2 * model_width + head_size, head_size),
        output_share,
        gain_share(model_width, model_width),
        shares[3],
        shares[4],
        down_share,
    )


def solution(mesh):
    return jax.shard_map(
        shards,
        mesh=mesh,
        in_specs=(
            P("dp", None),
            P("dp", None),
            P("dp", None),
            P(),
            P(None, "tensor"),
            P(None, "tensor"),
            P(None, "tensor"),
            P(),
            P(),
            P("tensor", None),
            P(),
            P(None, "tensor"),
            P(None, "tensor"),
            P("tensor", None),
            P("dp", None),
        ),
        out_specs=(
            P("dp", None),
            P("dp", None),
            P("dp"),
            P("dp", "tensor"),
            P("dp", "tensor"),
            P("dp", "tensor"),
            P("dp"),
            P("dp"),
            P("tensor", "dp"),
            P("dp"),
            P("dp", "tensor"),
            P("dp", "tensor"),
            P("tensor", "dp"),
        ),
        check_vma=False,
    )
```
